32 devices in a mesh: leaf: 4 (over y, core), wide: 8 (over z, x).
Axes of the slice: x: 2, y: 2, z: 4, core: 2. Of those that a mesh axis runs over, the one named last changes fastest.
Arguments:
- rhs: float32 [32768, 256], P(('leaf', 'wide')), may hold values from -6 to 6
- points: float32 [32768, 128], P(('leaf', 'wide')), may hold values from -6 to 6
- order: int32 [32768], P(('leaf', 'wide')), may hold values from 0 to 1023, as said below
- basis: float32 [32768, 256], P(('leaf', 'wide')), may hold values from -0.1875 to 0.1875
- transfer: float32 [32, 256, 256], P(('leaf', 'wide')), may hold values from -0.1875 to 0.1875
- skeleton: float32 [8, 256, 128], P('wide', 'leaf'), may hold values from -6 to 6
- far_ids: int32 [8, 6], replicated, may hold values from 0 to 7, as said below
- far_count: int32 [8], replicated, may hold values from 1 to 6
- near_ids: int32 [32, 2], P(('leaf', 'wide')), may hold values from 0 to 31, as said below
- near_count: int32 [32], P(('leaf', 'wide')), may hold values from 0 to 2
Outputs:
- product: float32 [32768, 256], P(('leaf', 'wide'))
The draws below stay inside these ranges and needn't reach their ends.
Inputs may be any that keep to these rules, and one draw needn't show every extreme that they name: `order`: within each leaf, the 1024 values are a permutation of 0 to 1023. `far_ids`: the first far_count[p] entries of row p are distinct parents other than p; later entries equal p. `near_ids`: the first near_count[g] entries of row g are distinct and each is g - 1 or g + 1 with the same leaf position, that is, a leaf of the parent beside g's parent; g - 1 comes first; later entries equal g.
All inputs are finite; a program needn't handle non-finite values.
Results may differ from the reference program's by a relative error of at most 0.0003.
Values sent between devices are 32-bit elements; how exact they have to be, the bound alone decides.
No kernel may reach another device: no remote copies, remote signals or barrier semaphores. Data moves between devices by JAX's collectives and lax.ppermute only.
A program may use at most 64 MiB of HBM per device.

```python
import jax
import jax.numpy as jnp
from jax import lax

LEAF = 1024
F = 128
RANK = 256
RHS = 256
FAR_MAX = 6
NEAR_MAX = 2
CHILDREN = 4
PARENTS = 8
LEAVES = 32
POINTS = 32768
N_LEAF = 4


def draw_order(key, part):
    keys = jax.random.split(key, LEAVES)
    perms = jax.vmap(lambda single: jax.random.permutation(single, LEAF))(keys)
    return perms.reshape(-1).astype(jnp.int32)


def far_table(key):
    keys = jax.random.split(jax.random.fold_in(key, 11), PARENTS)
    offsets = jax.vmap(lambda single: jax.random.permutation(single, PARENTS - 1)[:FAR_MAX])(keys) + 1
    rows = jnp.arange(PARENTS, dtype=jnp.int32)[:, None]
    ids = (rows + offsets.astype(jnp.int32)) % PARENTS
    counts = jax.random.randint(jax.random.fold_in(key, 12), (PARENTS,), 1, FAR_MAX + 1).astype(jnp.int32)
    counts = counts.at[0].set(FAR_MAX)
    slots = jnp.arange(FAR_MAX, dtype=jnp.int32)[None, :]
    ids = jnp.where(slots < counts[:, None], ids, rows)
    return (ids.astype(jnp.int32), counts)


def draw_far_ids(key, part):
    return far_table(key)[0]


def draw_far_count(key, part):
    return far_table(key)[1]


def near_table(key):
    numbers = jnp.arange(LEAVES, dtype=jnp.int32)
    position = numbers % PARENTS
    bits = jax.random.randint(jax.random.fold_in(key, 21), (LEAVES, 2), 0, 2).astype(jnp.int32)
    take_left = (position > 0) & (bits[:, 0] == 1)
    take_right = (position < PARENTS - 1) & (bits[:, 1] == 1)
    take_left = take_left | (numbers == 1)
    take_right = take_right | (numbers == 1)
    first = jnp.where(take_left, numbers - 1, jnp.where(take_right, numbers + 1, numbers))
    second = jnp.where(take_left & take_right, numbers + 1, numbers)
    counts = take_left.astype(jnp.int32) + take_right.astype(jnp.int32)
    return (jnp.stack([first, second], axis=1).astype(jnp.int32), counts)


def draw_near_ids(key, part):
    return near_table(key)[0]


def draw_near_count(key, part):
    return near_table(key)[1]


def steps_of(own_key, shape, cuts, least, high):
    def one(axis_at, blocks):
        draws = jax.random.uniform(jax.random.fold_in(jax.random.fold_in(own_key, 6), axis_at), (blocks,), jnp.float32, least / len(cuts), high / len(cuts))
        return jnp.repeat(jnp.exp(draws), shape[axis_at] // blocks).reshape((-1,) + (1,) * (len(shape) - axis_at - 1))

    level = one(*cuts[0])
    for cut in cuts[1:]:
        level = level * one(*cut)
    return level


def noise(own_key, dims, spread, reach, cuts=(), held_as=jnp.bfloat16):
    result = jax.random.normal(own_key, dims, jnp.float32) * spread
    if len(cuts) > 0:
        result = steps_of(own_key, dims, cuts, -0.22, 0.18) * result
    return jnp.clip(result, min=-reach, max=reach).astype(held_as)


def setup_inputs(seed: int = 0) -> dict:
    key_of = jax.random.split(jax.random.key(seed), 11)
    return {
        "rhs": noise(key_of[0], (POINTS, RHS), 1.0, 6.0, ((0, 32),), jnp.float32),
        "points": noise(key_of[1], (POINTS, F), 1.0, 6.0, ((0, 32),), jnp.float32),
        "order": draw_order(jax.random.fold_in(key_of[10], 71), 0),
        "basis": noise(key_of[3], (POINTS, RANK), LEAF ** -0.5, 0.1875, ((0, 32),), jnp.float32),
        "transfer": noise(key_of[4], (LEAVES, RANK, RANK), (RANK * CHILDREN) ** -0.5, 0.1875, ((0, 32),), jnp.float32),
        "skeleton": noise(key_of[5], (PARENTS, RANK, F), 1.0, 6.0, ((0, 8), (1, 4)), jnp.float32),
        "far_ids": draw_far_ids(jax.random.fold_in(key_of[10], 71), 0),
        "far_count": draw_far_count(jax.random.fold_in(key_of[10], 71), 0),
        "near_ids": draw_near_ids(jax.random.fold_in(key_of[10], 71), 0),
        "near_count": draw_near_count(jax.random.fold_in(key_of[10], 71), 0),
    }


HIGH = lax.Precision.HIGHEST


def multiply(left, right):
    return lax.dot_general(left, right, (((1,), (0,)), ((), ())), precision=HIGH, preferred_element_type=jnp.float32)


def kernel_tile(left, right):
    cross = lax.dot_general(left, right, (((1,), (1,)), ((), ())), precision=HIGH, preferred_element_type=jnp.float32)
    sq_left = jnp.sum(left * left, axis=1)
    sq_right = jnp.sum(right * right, axis=1)
    return jnp.exp((-2.0 / left.shape[1]) * (sq_left[:, None] + sq_right[None, :] - 2.0 * cross))


def reference(rhs, points, order, basis, transfer, skeleton, far_ids, far_count, near_ids, near_count):
    index = (jnp.arange(LEAVES, dtype=jnp.int32)[:, None] * LEAF + order.reshape(LEAVES, LEAF)).reshape(-1)
    tree_rhs = rhs[index]
    rhs_blocks = tree_rhs.reshape(LEAVES, LEAF, RHS)
    point_blocks = points.reshape(LEAVES, LEAF, F)
    basis_blocks = basis.reshape(LEAVES, LEAF, RANK)
    leaf_coef = jnp.einsum("lpr,lpc->lrc", basis_blocks, rhs_blocks, precision=HIGH)
    lifted = jnp.einsum("lrs,lrc->lsc", transfer, leaf_coef, precision=HIGH)
    parent_coef = jnp.sum(lifted.reshape(N_LEAF, PARENTS, RANK, RHS), axis=0)

    def far_one(parent):
        total = jnp.zeros((RANK, RHS), jnp.float32)
        for slot in range(FAR_MAX):
            other = far_ids[parent, slot]
            term = multiply(kernel_tile(skeleton[parent], skeleton[other]), parent_coef[other])
            total = total + jnp.where(slot < far_count[parent], term, jnp.float32(0.0))
        return total

    parent_field = lax.map(far_one, jnp.arange(PARENTS, dtype=jnp.int32))
    owners = jnp.arange(LEAVES, dtype=jnp.int32) % PARENTS
    leaf_field = jnp.einsum("lrs,lsc->lrc", transfer, parent_field[owners], precision=HIGH)

    def near_one(leaf_number):
        own_points = point_blocks[leaf_number]
        total = multiply(kernel_tile(own_points, own_points), rhs_blocks[leaf_number])
        for slot in range(NEAR_MAX):
            source = near_ids[leaf_number, slot]
            total = total + lax.cond(
                slot < near_count[leaf_number],
                lambda: multiply(kernel_tile(own_points, point_blocks[source]), rhs_blocks[source]),
                lambda: jnp.zeros((LEAF, RHS), jnp.float32))
        return total + multiply(basis_blocks[leaf_number], leaf_field[leaf_number])

    tree_out = lax.map(near_one, jnp.arange(LEAVES, dtype=jnp.int32)).reshape(POINTS, RHS)
    return jnp.zeros_like(rhs).at[index].set(tree_out)
```

```python
import functools
import math

import jax
import jax.numpy as jnp
from jax import lax
from jax.experimental import pallas as pl
from jax.experimental.pallas import tpu as pltpu
from jax.sharding import PartitionSpec as P

HIGH = lax.Precision.HIGH
BF = jnp.bfloat16
F32 = jnp.float32

def halves(x):
    hi=x.astype(BF); lo=(x-hi.astype(F32)).astype(BF)
    return hi,lo
def expand(x, second):
    f=x.shape[1]
    hi,lo=halves(x*F32(math.sqrt(4.0/f*math.log2(math.e))))
    hf=hi.astype(F32); lf=lo.astype(F32)
    n=jnp.sum(hf*(hf*0.5+lf),axis=1,keepdims=True)*-1.0
    a=n.astype(BF).astype(F32); b=(n-a).astype(BF).astype(F32); c=n-a-b
    lane=lax.broadcasted_iota(jnp.int32,x.shape,1)
    k=3 if second else 0
    ext=jnp.where(lane==k,a,jnp.where(lane==k+1,b,jnp.where(lane==k+2,c,jnp.where(lane<6,F32(1.0),F32(0.0)))))
    ext=ext.astype(BF)
    return jnp.concatenate([hi,hi,lo,ext] if second else [hi,lo,hi,ext],axis=1)
def mm(a,b): return lax.dot_general(a,b,(((1,),(0,)),((),())),preferred_element_type=F32)
def mmt(a,b): return lax.dot_general(a,b,(((1,),(1,)),((),())),preferred_element_type=F32)
def gauss_kernel(bm,bn,xa_ref,xb_ref,v_ref,o_ref,b4,vh,vl):
    @pl.when(pl.program_id(0)==0)
    def _():
        b4[...]=expand(xb_ref[...],True)
        h,l=halves(v_ref[...]); vh[...]=h; vl[...]=l
    a4=expand(xa_ref[...],False)
    n=xb_ref.shape[0]
    acc=None
    for j in range(n//bn):
        s=pl.ds(j*bn,bn)
        t=jnp.exp2(mmt(a4,b4[s,:]))
        th,tl=halves(t)
        part=mm(th,vh[s,:])+mm(tl,vh[s,:])+mm(th,vl[s,:])
        acc=part if acc is None else acc+part
    o_ref[...]=acc
def gauss_apply(xa,xb,v,bm=256, bn=256):
    m,f=xa.shape; n,c=v.shape
    return pl.pallas_call(functools.partial(gauss_kernel,bm,bn),
        out_shape=jax.ShapeDtypeStruct((m,c),F32),
        grid=(m//bm,),
        in_specs=[pl.BlockSpec((bm,f),lambda i:(i,0)),pl.BlockSpec((n,f),lambda i:(0,0)),pl.BlockSpec((n,c),lambda i:(0,0))],
        out_specs=pl.BlockSpec((bm,c),lambda i:(i,0)),
        scratch_shapes=[pltpu.VMEM((n,4*f),BF),pltpu.VMEM((n,c),BF),pltpu.VMEM((n,c),BF)],
        cost_estimate=pl.CostEstimate(flops=2*m*n*(4*f+3*c),bytes_accessed=4*(m*f+n*f+n*c+m*c),transcendentals=m*n),
    )(xa,xb,v)
def permute_kernel(order_ref,x_ref,w_ref,xo_ref,wo_ref,xs,ws):
    f=x_ref.shape[1]; c=w_ref.shape[1]; bm=xo_ref.shape[0]; n=x_ref.shape[0]
    @pl.when(pl.program_id(0)==0)
    def _():
        h,l=halves(x_ref[...]); xs[:,:f]=h; xs[:,f:]=l
        h,l=halves(w_ref[...]); ws[:,:c]=h; ws[:,c:]=l
    row=lax.broadcasted_iota(jnp.int32,(bm,n),0)+pl.program_id(0)*bm
    hot=jnp.where(row==order_ref[...],F32(1.0),F32(0.0)).astype(BF)
    p=mm(hot,xs[...]); xo_ref[...]=p[:,:f]+p[:,f:]
    p=mm(hot,ws[...]); wo_ref[...]=p[:,:c]+p[:,c:]
def permute(order,x,w,bm=256):
    n,f=x.shape; c=w.shape[1]
    return pl.pallas_call(permute_kernel,
        out_shape=(jax.ShapeDtypeStruct((n,f),F32),jax.ShapeDtypeStruct((n,c),F32)),
        grid=(n//bm,),
        in_specs=[pl.BlockSpec((1,n),lambda i:(0,0)),pl.BlockSpec((n,f),lambda i:(0,0)),pl.BlockSpec((n,c),lambda i:(0,0))],
        out_specs=(pl.BlockSpec((bm,f),lambda i:(i,0)),pl.BlockSpec((bm,c),lambda i:(i,0))),
        scratch_shapes=[pltpu.VMEM((n,2*f),BF),pltpu.VMEM((n,2*c),BF)],
        cost_estimate=pl.CostEstimate(flops=2*n*n*2*(f+c),bytes_accessed=8*n*(f+c),transcendentals=0),
    )(order.reshape(1,n),x,w)


def passed_along(block, axis, distance):
    devices = range(lax.axis_size(axis))
    route = [(i - distance, i) for i in devices if i - distance in devices]
    return lax.ppermute(block, axis, route)


def multiply(left, right):
    return lax.dot_general(left, right, (((1,), (0,)), ((), ())), precision=HIGH, preferred_element_type=F32)


def multiply_first(left, right):
    return lax.dot_general(left, right, (((0,), (0,)), ((), ())), precision=HIGH, preferred_element_type=F32)


def after(value, *others):
    return lax.optimization_barrier((value,) + others)[0]


def every_parent(block):
    count = lax.axis_size("wide")
    me = lax.axis_index("wide")
    other = lax.ppermute(block, "wide", [(i, i ^ 1) for i in range(count)])
    even = me % 2 == 0
    pair = jnp.stack([jnp.where(even, block, other), jnp.where(even, other, block)])
    pairs = [pair]
    for k in range(1, count // 2):
        pairs.append(lax.ppermute(pair, "wide", [(i, (i + 2 * k) % count) for i in range(count)]))
    number = jnp.arange(count, dtype=jnp.int32)
    number = (me - me % 2 - 2 * (number // 2)) % count + number % 2
    return jnp.concatenate(pairs), number


def shards(rhs, points, order, basis, transfer, skeleton, far_ids, far_count, near_ids, near_count):
    wide_count = lax.axis_size("wide")
    leaf_count = lax.axis_size("leaf")
    parent = lax.axis_index("wide")
    leaf_number = lax.axis_index("leaf") * wide_count + parent
    size, cols = rhs.shape
    half = size // 2
    own_transfer = transfer[0]
    near_row = near_ids[0]
    used = jnp.arange(near_row.shape[0], dtype=jnp.int32) < near_count[0]
    has_left = jnp.any(used & (near_row == leaf_number - 1))
    has_right = jnp.any(used & (near_row == leaf_number + 1))

    right_first = passed_along(rhs[:half], "wide", -1)
    spots, rows = permute(order, points, basis, 512)
    right_spots = passed_along(spots, "wide", -1)

    lifted = multiply_first(own_transfer, multiply_first(rows, rhs))
    skel = skeleton[0]
    parts = jnp.concatenate(
        [lifted.reshape(leaf_count, -1, cols), jnp.broadcast_to(skel[None], (leaf_count,) + skel.shape)], axis=2
    )
    parts = lax.all_to_all(parts, "leaf", 0, 0)
    skel_full = parts[:, :, cols:].reshape(-1, skel.shape[1])
    block = jnp.concatenate([jnp.sum(parts[:, :, :cols], axis=0), skel], axis=1)
    blocks, number = every_parent(block)
    right_second = passed_along(after(rhs[half:], right_spots, block), "wide", -1)
    slots = jnp.arange(far_ids.shape[1], dtype=jnp.int32) < far_count[parent]
    wanted = jnp.any(slots[None, :] & (far_ids[parent][None, :] == number[:, None]), axis=1)
    coefs = jnp.where(wanted[:, None, None], blocks[:, :, :cols], F32(0.0)).reshape(-1, cols)
    field = gauss_apply(skel_full, blocks[:, :, cols:].reshape(-1, skel.shape[1]), coefs)
    field = jnp.sum(lax.all_to_all(field.reshape(leaf_count, -1, cols), "leaf", 0, 0), axis=0)
    field = lax.all_gather(field, "leaf", axis=0, tiled=True)
    far_out = multiply(rows, multiply(own_transfer, field))

    returned = gauss_apply(right_spots, spots, rhs, 1024)
    left_share = passed_along(returned, "wide", 1)
    total = gauss_apply(spots, spots, rhs, 1024)
    first = gauss_apply(spots, right_spots[:half], right_first, 1024)
    second = gauss_apply(spots, right_spots[half:], right_second, 1024)
    total = total + jnp.where(has_right, first + second, F32(0.0))
    total = total + far_out
    return total + jnp.where(has_left, left_share, F32(0.0))


def solution(mesh):
    placed = (
        P(("leaf", "wide"), None),
        P(("leaf", "wide"), None),
        P(("leaf", "wide")),
        P(("leaf", "wide"), None),
        P(("leaf", "wide"), None, None),
        P("wide", "leaf", None),
        P(),
        P(),
        P(("leaf", "wide"), None),
        P(("leaf", "wide")),
    )
    return jax.shard_map(
        shards, mesh=mesh, in_specs=placed, out_specs=P(("leaf", "wide"), None), check_vma=False
    )
```

```python
import functools
import math

import jax
import jax.numpy as jnp
from jax import lax
from jax.experimental import pallas as pl
from jax.experimental.pallas import tpu as pltpu
from jax.sharding import PartitionSpec as P

BF = jnp.bfloat16
F32 = jnp.float32
VMEM_BYTES = 28 << 20


def halves(x):
    hi = x.astype(BF)
    return hi, (x - hi.astype(F32)).astype(BF)


def expand(x, second):
    features = x.shape[1]
    hi, lo = halves(x * F32(math.sqrt(4.0 / features * math.log2(math.e))))
    hi_wide = hi.astype(F32)
    norm = jnp.sum(hi_wide * (hi_wide * 0.5 + lo.astype(F32)), axis=1, keepdims=True) * -1.0
    a = norm.astype(BF).astype(F32)
    b = (norm - a).astype(BF).astype(F32)
    c = norm - a - b
    lane = lax.broadcasted_iota(jnp.int32, x.shape, 1)
    k = 3 if second else 0
    ones = jnp.where(lane < 6, F32(1.0), F32(0.0))
    ext = jnp.where(lane == k, a, jnp.where(lane == k + 1, b, jnp.where(lane == k + 2, c, ones))).astype(BF)
    return jnp.concatenate([hi, hi, lo, ext] if second else [hi, lo, hi, ext], axis=1)


def dot(left, right):
    return lax.dot_general(left, right, (((1,), (0,)), ((), ())), preferred_element_type=F32)


def dot_last(left, right):
    return lax.dot_general(left, right, (((1,), (1,)), ((), ())), preferred_element_type=F32)


def dot_first(left, right):
    return lax.dot_general(left, right, (((0,), (0,)), ((), ())), preferred_element_type=F32)


def product(left, right, op=dot):
    lh, ll = halves(left)
    rh, rl = halves(right)
    return op(lh, rh) + op(ll, rh) + op(lh, rl)


def tile_product(targets, sources, value_hi, value_lo, step):
    total = None
    for start in range(0, sources.shape[0], step):
        span = pl.ds(start, step)
        hi, lo = halves(jnp.exp2(dot_last(targets, sources[span, :])))
        part = dot(hi, value_hi[span, :]) + dot(lo, value_hi[span, :]) + dot(hi, value_lo[span, :])
        total = part if total is None else total + part
    return total


def step_of(count):
    return 256 if count % 256 == 0 else count


def near_flag(near_ids, near_count, offset):
    wide = lax.axis_size("wide")
    wanted = lax.axis_index("leaf") * wide + lax.axis_index("wide") + offset
    found = jnp.int32(0)
    for slot in range(near_ids.shape[1]):
        hit = (near_ids[0, slot] == wanted) & (slot < near_count[0])
        found = found | hit.astype(jnp.int32)
    return found > 0


def hot_rows(order_ref):
    n = order_ref.shape[1]
    row = lax.broadcasted_iota(jnp.int32, (n, n), 0)
    return jnp.where(row == order_ref[...], F32(1.0), F32(0.0)).astype(BF)


def spots_kernel(order_ref, x_ref, o_ref):
    hi, lo = halves(x_ref[...])
    hot = hot_rows(order_ref)
    width = x_ref.shape[1]
    both = dot(hot, jnp.concatenate([hi, lo], axis=1))
    o_ref[...] = both[:, :width] + both[:, width:]


def coef_kernel(order_ref, w_ref, v_ref, t_ref, s_ref, rows_ref, parts_ref):
    hi, lo = halves(w_ref[...])
    hot = hot_rows(order_ref)
    rows = dot(hot, hi)
    rows_lo = dot(hot, lo)
    rows_ref[...] = rows + rows_lo
    rh, rl = rows.astype(BF), rows_lo.astype(BF)
    vh, vl = halves(v_ref[...])
    coef = dot_first(rh, vh) + dot_first(rl, vh) + dot_first(rh, vl)
    lifted = product(t_ref[0], coef, dot_first)
    blocks, block, _ = parts_ref.shape
    cols = v_ref.shape[1]
    for k in range(blocks):
        parts_ref[k, :, :cols] = lifted[k * block : (k + 1) * block]
        parts_ref[k, :, cols:] = s_ref[0]


def gather_kernel(parts_ref, s_ref, o_ref):
    cols = o_ref.shape[1] - s_ref.shape[2]
    total = parts_ref[0, :, :cols]
    for k in range(1, parts_ref.shape[0]):
        total = total + parts_ref[k, :, :cols]
    o_ref[:, :cols] = total
    o_ref[:, cols:] = s_ref[0]


def self_kernel(x_ref, v_ref, o_ref, wide, vh, vl):
    x = x_ref[...]
    wide[...] = expand(x, True)
    vh[...], vl[...] = halves(v_ref[...])
    o_ref[...] = tile_product(expand(x, False), wide, vh, vl, step_of(v_ref.shape[0]))


def returned_kernel(xh_ref, x_ref, v_ref, o_ref, wide, vh, vl):
    wide[...] = expand(x_ref[...], True)
    vh[...], vl[...] = halves(v_ref[...])
    o_ref[...] = tile_product(expand(xh_ref[...], False), wide, vh, vl, step_of(v_ref.shape[0]))


def own_kernel(ids_ref, count_ref, total_ref, x_ref, xh_ref, va_ref, vb_ref, o_ref, wide, vh, vl):
    has_right = near_flag(ids_ref, count_ref, 1)
    first = va_ref.shape[0]

    @pl.when(has_right)
    def _():
        wide[...] = expand(xh_ref[...], True)
        vh[:first, :], vl[:first, :] = halves(va_ref[...])
        vh[first:, :], vl[first:, :] = halves(vb_ref[...])
        o_ref[...] = total_ref[...] + tile_product(expand(x_ref[...], False), wide, vh, vl, step_of(wide.shape[0]))

    @pl.when(jnp.logical_not(has_right))
    def _():
        o_ref[...] = total_ref[...]


def far_kernel(pairs, ids_ref, count_ref, parts_ref, *refs):
    block_refs, (o_ref, wide, vh, vl) = refs[:pairs], refs[pairs:]
    cols = o_ref.shape[2]
    rows = parts_ref.shape[1]
    me = lax.axis_index("wide")
    parents = 2 * pairs
    pair = me // 2
    for k in range(pairs):
        for side in range(2):
            other = 2 * lax.rem(pair - k + pairs, pairs) + side
            wanted = jnp.int32(0)
            for slot in range(ids_ref.shape[1]):
                hit = (ids_ref[me, slot] == other) & (slot < count_ref[me])
                wanted = wanted | hit.astype(jnp.int32)
            span = pl.ds((2 * k + side) * rows, rows)
            wide[span, :] = expand(block_refs[k][side, :, cols:], True)
            hi, lo = halves(jnp.where(wanted > 0, block_refs[k][side, :, :cols], F32(0.0)))
            vh[span, :] = hi
            vl[span, :] = lo
    targets = jnp.concatenate([expand(parts_ref[k, :, cols:], False) for k in range(parts_ref.shape[0])], axis=0)
    field = tile_product(targets, wide, vh, vl, step_of(parents * rows))
    for k in range(o_ref.shape[0]):
        o_ref[k] = field[k * rows : (k + 1) * rows]


def block_sum_kernel(parts_ref, o_ref):
    total = parts_ref[0]
    for k in range(1, parts_ref.shape[0]):
        total = total + parts_ref[k]
    o_ref[...] = total


def lower_kernel(total_ref, rows_ref, t_ref, f_ref, o_ref):
    leaf_field = product(t_ref[0], f_ref[...])
    o_ref[...] = total_ref[...] + product(rows_ref[...], leaf_field)


def last_kernel(ids_ref, count_ref, total_ref, share_ref, o_ref):
    has_left = near_flag(ids_ref, count_ref, -1)
    o_ref[...] = total_ref[...] + jnp.where(has_left, share_ref[...], F32(0.0))


VM = pl.BlockSpec(memory_space=pltpu.VMEM)
SM = pl.BlockSpec(memory_space=pltpu.SMEM)


def kernel_call(body, out, args, specs, scratch=(), flops=0):
    moved = sum(a.size for a in args) * 4
    many = isinstance(out[0], tuple)
    outs = out if many else (out,)
    shapes = tuple(jax.ShapeDtypeStruct(s, F32) for s in outs)
    return pl.pallas_call(
        body,
        out_shape=shapes if many else shapes[0],
        in_specs=specs,
        out_specs=tuple(VM for _ in outs) if many else VM,
        scratch_shapes=list(scratch),
        compiler_params=pltpu.CompilerParams(vmem_limit_bytes=VMEM_BYTES),
        cost_estimate=pl.CostEstimate(flops=flops, bytes_accessed=moved, transcendentals=0),
    )(*args)


def passed_along(block, distance):
    devices = range(lax.axis_size("wide"))
    route = [(i - distance, i) for i in devices if i - distance in devices]
    return lax.ppermute(block, "wide", route)


def shards(rhs, points, order, basis, transfer, skeleton, far_ids, far_count, near_ids, near_count):
    wide = lax.axis_size("wide")
    leaf = lax.axis_size("leaf")
    me = lax.axis_index("wide")
    size, cols = rhs.shape
    features = points.shape[1]
    rank = transfer.shape[1]
    rows = rank // leaf
    order = order.reshape(1, size)
    start = size // 8
    tile_flops = 2 * size * size * (4 * features + 3 * cols)
    scratch = [pltpu.VMEM((size, 4 * features), BF), pltpu.VMEM((size, cols), BF), pltpu.VMEM((size, cols), BF)]

    right_first = passed_along(rhs[:start], -1)
    spots = kernel_call(spots_kernel, (size, features), (order, points), [VM] * 2, (), 4 * size * size * features)
    right_spots = passed_along(spots, -1)
    basis_rows, parts = kernel_call(
        coef_kernel, ((size, rank), (leaf, rows, cols + features)),
        (order, basis, rhs, transfer, skeleton), [VM] * 5, (), 4 * size * size * rank,
    )
    parts = lax.all_to_all(parts, "leaf", 0, 0)
    total = kernel_call(self_kernel, (size, cols), (spots, rhs), [VM] * 2, scratch, tile_flops)
    block = kernel_call(gather_kernel, (rows, cols + features), (parts, skeleton), [VM] * 2)
    other = lax.ppermute(block, "wide", [(i, i ^ 1) for i in range(wide)])
    right_second = passed_along(rhs[start:], -1)
    even = me % 2 == 0
    pair = jnp.stack([jnp.where(even, block, other), jnp.where(even, other, block)])
    pairs = [pair]
    for k in range(1, wide // 2):
        pairs.append(lax.ppermute(pair, "wide", [(i, (i + 2 * k) % wide) for i in range(wide)]))

    returned = kernel_call(returned_kernel, (size, cols), (right_spots, spots, rhs), [VM] * 3, scratch, tile_flops)
    left_share = passed_along(returned, 1)

    far_scratch = [
        pltpu.VMEM((wide * rows, 4 * features), BF), pltpu.VMEM((wide * rows, cols), BF), pltpu.VMEM((wide * rows, cols), BF)
    ]
    field = kernel_call(
        functools.partial(far_kernel, len(pairs)), (leaf, rows, cols), (far_ids, far_count, parts, *pairs),
        [SM, SM] + [VM] * (1 + len(pairs)), far_scratch, 2 * rank * rows * wide * (4 * features + 3 * cols),
    )
    field = lax.all_to_all(field, "leaf", 0, 0)
    field = kernel_call(block_sum_kernel, (rows, cols), (field,), [VM])
    field = lax.all_gather(field, "leaf", axis=0, tiled=True)
    total = kernel_call(
        own_kernel, (size, cols), (near_ids, near_count, total, spots, right_spots, right_first, right_second),
        [SM, SM] + [VM] * 5, scratch, tile_flops,
    )
    total = kernel_call(lower_kernel, (size, cols), (total, basis_rows, transfer, field), [VM] * 4, (), 6 * size * rank * cols)
    return kernel_call(last_kernel, (size, cols), (near_ids, near_count, total, left_share), [SM, SM] + [VM] * 2)


def solution(mesh):
    placed = (
        P(("leaf", "wide"), None),
        P(("leaf", "wide"), None),
        P(("leaf", "wide")),
        P(("leaf", "wide"), None),
        P(("leaf", "wide"), None, None),
        P("wide", "leaf", None),
        P(),
        P(),
        P(("leaf", "wide"), None),
        P(("leaf", "wide")),
    )
    return jax.shard_map(shards, mesh=mesh, in_specs=placed, out_specs=P(("leaf", "wide"), None), check_vma=False)
```

```python
import functools
import math

import jax
import jax.numpy as jnp
from jax import lax
from jax.experimental import pallas as pl
from jax.experimental.pallas import tpu as pltpu
from jax.sharding import PartitionSpec as P

BF = jnp.bfloat16
F32 = jnp.float32
VMEM_BYTES = 28 << 20


def halves(x):
    hi = x.astype(BF)
    return hi, (x - hi.astype(F32)).astype(BF)


def expand(x, second):
    features = x.shape[1]
    hi, lo = halves(x * F32(math.sqrt(4.0 / features * math.log2(math.e))))
    hi_wide = hi.astype(F32)
    norm = jnp.sum(hi_wide * (hi_wide * 0.5 + lo.astype(F32)), axis=1, keepdims=True) * -1.0
    a = norm.astype(BF).astype(F32)
    b = (norm - a).astype(BF).astype(F32)
    c = norm - a - b
    lane = lax.broadcasted_iota(jnp.int32, x.shape, 1)
    k = 3 if second else 0
    ones = jnp.where(lane < 6, F32(1.0), F32(0.0))
    ext = jnp.where(lane == k, a, jnp.where(lane == k + 1, b, jnp.where(lane == k + 2, c, ones))).astype(BF)
    return jnp.concatenate([hi, hi, lo, ext] if second else [hi, lo, hi, ext], axis=1)


def dot(left, right):
    return lax.dot_general(left, right, (((1,), (0,)), ((), ())), preferred_element_type=F32)


def dot_last(left, right):
    return lax.dot_general(left, right, (((1,), (1,)), ((), ())), preferred_element_type=F32)


def dot_first(left, right):
    return lax.dot_general(left, right, (((0,), (0,)), ((), ())), preferred_element_type=F32)


def product(left, right, op=dot):
    lh, ll = halves(left)
    rh, rl = halves(right)
    return op(lh, rh) + op(ll, rh) + op(lh, rl)


def tile_product(targets, sources, value_hi, value_lo, step):
    total = None
    for start in range(0, sources.shape[0], step):
        span = pl.ds(start, step)
        hi, lo = halves(jnp.exp2(dot_last(targets, sources[span, :])))
        part = dot(hi, value_hi[span, :]) + dot(lo, value_hi[span, :]) + dot(hi, value_lo[span, :])
        total = part if total is None else total + part
    return total


def step_of(count):
    return 256 if count % 256 == 0 else count


def near_flag(near_ids, near_count, offset):
    wide = lax.axis_size("wide")
    wanted = lax.axis_index("leaf") * wide + lax.axis_index("wide") + offset
    found = jnp.int32(0)
    for slot in range(near_ids.shape[1]):
        hit = (near_ids[0, slot] == wanted) & (slot < near_count[0])
        found = found | hit.astype(jnp.int32)
    return found > 0


def hot_rows(order_ref):
    n = order_ref.shape[1]
    row = lax.broadcasted_iota(jnp.int32, (n, n), 0)
    return jnp.where(row == order_ref[...], F32(1.0), F32(0.0)).astype(BF)


def fetch(pairs, sems):
    copies = [pltpu.make_async_copy(src, dst, sems.at[k]) for k, (src, dst) in enumerate(pairs)]
    for copy in copies:
        copy.start()
    return copies


def front_kernel(order_hbm, x_hbm, w_hbm, v_hbm, t_hbm, s_hbm, spots_ref, rows_ref, sum_ref, va_ref, vb_ref, order_ref, x, w, v, t, s, sems):
    first, *copies = fetch(
        ((order_hbm, order_ref), (x_hbm, x), (w_hbm, w), (v_hbm, v), (t_hbm, t), (s_hbm, s)), sems
    )
    first.wait()
    hot = hot_rows(order_ref)
    width = x.shape[1]
    copies[0].wait()
    hi, lo = halves(x[...])
    both = dot(hot, jnp.concatenate([hi, lo], axis=1))
    spots_ref[...] = both[:, :width] + both[:, width:]
    copies[1].wait()
    hi, lo = halves(w[...])
    rows = dot(hot, hi)
    rows_lo = dot(hot, lo)
    rows_ref[...] = rows + rows_lo
    rh, rl = rows.astype(BF), rows_lo.astype(BF)
    copies[2].wait()
    half = va_ref.shape[0]
    va_ref[...] = v[:half, :]
    vb_ref[...] = v[half:, :]
    vh, vl = halves(v[...])
    coef = dot_first(rh, vh) + dot_first(rl, vh) + dot_first(rh, vl)
    copies[3].wait()
    copies[4].wait()
    rank = t.shape[1]
    sum_ref[:rank, :] = product(t[0], coef, dot_first)
    sum_ref[rank:, : s.shape[2]] = s[0]
    sum_ref[rank:, s.shape[2] :] = s[0]


def chip_kernel(own_ref, mate_ref, keep_ref, *send_refs):
    leaf = lax.axis_index("leaf")
    chips = len(send_refs) + 1
    features = (keep_ref.shape[1] - own_ref.shape[1]) // 2
    cols = own_ref.shape[1]
    block = keep_ref.shape[0]
    rank = own_ref.shape[0] - block
    for shift, ref in enumerate((keep_ref,) + send_refs):
        chip = lax.rem(leaf // 2 + shift, chips)
        span = pl.ds(pl.multiple_of((2 * chip + leaf % 2) * block, block), block)
        ref[:, :cols] = own_ref[span, :] + mate_ref[span, :]
        ref[:, cols : cols + features] = own_ref[rank:, :features]
        ref[:, cols + features :] = mate_ref[rank:, :features]


def gather_kernel(*refs):
    received, (block_ref, skel_ref) = refs[:-2], refs[-2:]
    leaf = lax.axis_index("leaf")
    chips = len(received)
    features = skel_ref.shape[1]
    cols = block_ref.shape[1] - features
    block = block_ref.shape[0]
    total = received[0][:, :cols]
    for ref in received[1:]:
        total = total + ref[:, :cols]
    block_ref[:, :cols] = total
    block_ref[:, cols:] = received[0][:, cols : cols + features]
    core = leaf % 2
    for shift, ref in enumerate(received):
        chip = lax.rem(leaf // 2 - shift + chips, chips)
        same = pl.multiple_of((2 * chip + core) * block, block)
        mate = pl.multiple_of((2 * chip + 1 - core) * block, block)
        skel_ref[pl.ds(same, block), :] = ref[:, cols : cols + features]
        skel_ref[pl.ds(mate, block), :] = ref[:, cols + features :]


def pair_kernel(block_ref, other_ref, o_ref):
    even = lax.axis_index("wide") % 2 == 0
    o_ref[0] = jnp.where(even, block_ref[...], other_ref[...])
    o_ref[1] = jnp.where(even, other_ref[...], block_ref[...])


def self_kernel(x_ref, v_hbm, o_ref, v, wide, vh, vl, sems):
    copies = fetch(((v_hbm, v),), sems)
    x = x_ref[...]
    wide[...] = expand(x, True)
    targets = expand(x, False)
    copies[0].wait()
    vh[...], vl[...] = halves(v[...])
    o_ref[...] = tile_product(targets, wide, vh, vl, step_of(v.shape[0]))


def is_heavy():
    return (lax.axis_index("wide") + lax.axis_index("leaf")) % 2 == 0


def sides():
    partner = 1 - 2 * (lax.axis_index("wide") % 2)
    return partner, -partner


def pair_product_kernel(heavy, a_ref, b_ref, *refs):
    v_refs, (o_ref, wide, vh, vl) = refs[:-4], refs[-4:]

    @pl.when(is_heavy() == heavy)
    def _():
        wide[...] = expand(b_ref[...], True)
        targets = expand(a_ref[...], False)
        start = 0
        for ref in v_refs:
            span = pl.ds(start, ref.shape[0])
            vh[span, :], vl[span, :] = halves(ref[...])
            start += ref.shape[0]
        o_ref[...] = tile_product(targets, wide, vh, vl, step_of(vh.shape[0]))


def far_kernel(pairs, ids_hbm, count_hbm, skel_ref, *refs):
    block_refs, (o_ref, wide, vh, vl, ids_ref, count_ref, sems) = refs[:pairs], refs[pairs:]
    copies = fetch(((ids_hbm, ids_ref), (count_hbm, count_ref)), sems)
    cols = o_ref.shape[1]
    rows = block_refs[0].shape[1]
    me = lax.axis_index("wide")
    pair = me // 2
    for k in range(pairs):
        for side in range(2):
            wide[pl.ds((2 * k + side) * rows, rows), :] = expand(block_refs[k][side, :, cols:], True)
    targets = expand(skel_ref[...], False)
    for copy in copies:
        copy.wait()
    for k in range(pairs):
        for side in range(2):
            other = 2 * lax.rem(pair - k + pairs, pairs) + side
            wanted = jnp.int32(0)
            for slot in range(ids_ref.shape[1]):
                hit = (ids_ref[me, slot] == other) & (slot < count_ref[me])
                wanted = wanted | hit.astype(jnp.int32)
            span = pl.ds((2 * k + side) * rows, rows)
            hi, lo = halves(jnp.where(wanted > 0, block_refs[k][side, :, :cols], F32(0.0)))
            vh[span, :] = hi
            vl[span, :] = lo
    o_ref[...] = tile_product(targets, wide, vh, vl, step_of(2 * pairs * rows))


def add_kernel(a_ref, b_ref, o_ref):
    o_ref[...] = a_ref[...] + b_ref[...]


def last_kernel(chips, ids_ref, count_ref, total, rows, t, near_ref, far_ref, own_ref, mine_ref, *refs):
    field_refs, (kept_ref, o_hbm, out, sems) = refs[:chips], refs[chips:]
    heavy = is_heavy()
    partner, other = sides()
    to_partner = near_flag(ids_ref, count_ref, partner)
    to_other = near_flag(ids_ref, count_ref, other)
    field = kept_ref[...]
    for ref in field_refs:
        field = field + ref[...]
    lh, ll = halves(product(t[0], field))
    step = step_of(out.shape[0])
    stores = []
    for k in range(out.shape[0] // step):
        span = pl.ds(k * step, step)
        rh, rl = halves(rows[span, :])
        block = total[span, :] + dot(rh, lh) + dot(rl, lh) + dot(rh, ll)
        first = jnp.where(heavy, mine_ref[span, :], near_ref[span, :])
        second = jnp.where(heavy, own_ref[span, :], far_ref[span, :])
        block = block + jnp.where(to_partner, first, F32(0.0))
        out[span, :] = block + jnp.where(to_other, second, F32(0.0))
        stores.append(pltpu.make_async_copy(out.at[span, :], o_hbm.at[span, :], sems.at[k]))
        stores[-1].start()
    for store in stores:
        store.wait()


VM = pl.BlockSpec(memory_space=pltpu.VMEM)
SM = pl.BlockSpec(memory_space=pltpu.SMEM)
ANY = pl.BlockSpec(memory_space=pl.ANY)
HBM = pl.BlockSpec(memory_space=pltpu.HBM)


def kernel_call(body, out, args, specs, scratch=(), flops=0, out_spec=VM):
    many = isinstance(out[0], tuple)
    outs = out if many else (out,)
    moved = 4 * (sum(a.size for a in args) + sum(math.prod(o) for o in outs))
    shapes = tuple(jax.ShapeDtypeStruct(s, F32) for s in outs)
    return pl.pallas_call(
        body,
        out_shape=shapes if many else shapes[0],
        in_specs=specs,
        out_specs=tuple(out_spec for _ in outs) if many else out_spec,
        scratch_shapes=list(scratch),
        compiler_params=pltpu.CompilerParams(vmem_limit_bytes=VMEM_BYTES),
        cost_estimate=pl.CostEstimate(flops=flops, bytes_accessed=moved, transcendentals=0),
    )(*args)


def sent(block, route):
    return lax.ppermute(block, ("leaf", "wide"), route)


def routes(leaf, wide):
    swap, onward, back, back_far, to_mate = [], [], [], [], []
    for l in range(leaf):
        step = -2 if l % 2 else 2
        for p in range(wide):
            here, mate, partner = l * wide + p, (l ^ 1) * wide + p, l * wide + (p ^ 1)
            if (l + p) % 2:
                swap.append((here, partner))
                continue
            swap.append((here, mate))
            back.append((here, partner))
            to_mate.append((mate, here))
            if 0 <= p + step < wide:
                onward.append((here, mate + step))
            if 0 <= p - step // 2 < wide:
                back_far.append((mate, here - step // 2))
    return swap, onward, back, back_far, to_mate


def shards(rhs, points, order, basis, transfer, skeleton, far_ids, far_count, near_ids, near_count):
    wide = lax.axis_size("wide")
    leaf = lax.axis_size("leaf")
    chips = leaf // 2
    size, cols = rhs.shape
    features = points.shape[1]
    rank = transfer.shape[1]
    rows = rank // leaf
    order = order.reshape(1, size)
    swap, onward, back, back_far, to_mate = routes(leaf, wide)
    all_wide = lambda move: [(l * wide + p, move(l, p)) for l in range(leaf) for p in range(wide)]
    mates = all_wide(lambda l, p: (l ^ 1) * wide + p)
    partners = all_wide(lambda l, p: l * wide + (p ^ 1))
    tile_flops = 2 * size * size * (4 * features + 3 * cols)
    dma = pltpu.SemaphoreType.DMA
    spot_buf, rhs_buf = pltpu.VMEM((size, features), F32), pltpu.VMEM((size, cols), F32)
    scratch = [pltpu.VMEM((size, 4 * features), BF), pltpu.VMEM((size, cols), BF), pltpu.VMEM((size, cols), BF)]

    def across_chips(blocks):
        return [
            sent(block, all_wide(lambda l, p: ((l // 2 + shift) % chips * 2 + l % 2) * wide + p))
            for shift, block in enumerate(blocks, 1)
        ]

    def pair_product(heavy, a, b, *v):
        return kernel_call(
            functools.partial(pair_product_kernel, heavy), (size, cols), (a, b) + v, [VM] * (2 + len(v)),
            scratch, tile_flops,
        )

    half = size // 2
    spots, basis_rows, term, rhs_a, rhs_b = kernel_call(
        front_kernel, ((size, features), (size, rank), (rank + rows, cols), (half, cols), (size - half, cols)),
        tuple(pltpu.with_memory_space_constraint(t, pltpu.HBM) for t in (order, points, basis, rhs, transfer, skeleton)),
        [HBM] * 6,
        [pltpu.VMEM((1, size), jnp.int32), spot_buf, pltpu.VMEM((size, rank), F32), rhs_buf, pltpu.VMEM(transfer.shape, F32), pltpu.VMEM(skeleton.shape, F32), dma((6,))],
        4 * size * size * (rank + features),
    )
    mate_term = sent(term, mates)
    spots_in = sent(spots, swap)
    kept, *sends = kernel_call(chip_kernel, ((rows, cols + 2 * features),) * chips, (term, mate_term), [VM] * 2)
    received = across_chips(sends)
    total = kernel_call(self_kernel, (size, cols), (spots, rhs), [VM, ANY], [rhs_buf] + scratch + [dma((1,))], tile_flops)
    block, skel = kernel_call(
        gather_kernel, ((rows, cols + features), (rank, features)), (kept, *received), [VM] * chips
    )
    other = sent(block, partners)
    rhs_in = (sent(rhs_a, swap), sent(rhs_b, swap))
    spots_far = sent(spots_in, onward)
    pair = kernel_call(pair_kernel, (2,) + block.shape, (block, other), [VM] * 2)
    pairs = [pair] + [sent(pair, all_wide(lambda l, p: l * wide + (p + 2 * k) % wide)) for k in range(1, wide // 2)]
    share_near = sent(pair_product(True, spots_in, spots, rhs), back)
    share_far = sent(pair_product(False, spots_far, spots_in, *rhs_in), back_far)
    rhs_far = (sent(rhs_in[0], onward), sent(rhs_in[1], onward))
    mine = pair_product(True, spots, spots_in, *rhs_in)
    field = kernel_call(
        functools.partial(far_kernel, len(pairs)), (rank, cols),
        (pltpu.with_memory_space_constraint(far_ids, pltpu.HBM), pltpu.with_memory_space_constraint(far_count, pltpu.HBM), skel, *pairs),
        [HBM, HBM] + [VM] * (1 + len(pairs)),
        [pltpu.VMEM((wide * rows, 4 * features), BF), pltpu.VMEM((wide * rows, cols), BF), pltpu.VMEM((wide * rows, cols), BF)]
        + [pltpu.SMEM(far_ids.shape, jnp.int32), pltpu.SMEM(far_count.shape, jnp.int32), dma((2,))],
        2 * rank * rows * wide * (4 * features + 3 * cols),
    )
    mate_field = sent(field, mates)
    field = kernel_call(add_kernel, (rank, cols), (field, mate_field), [VM] * 2)
    fields = across_chips([field] * (chips - 1))
    own_far = sent(pair_product(False, spots_in, spots_far, *rhs_far), to_mate)
    return kernel_call(
        functools.partial(last_kernel, chips - 1), (size, cols),
        (near_ids, near_count, total, basis_rows, transfer, share_near, share_far, own_far, mine, *fields, field),
        [SM, SM] + [VM] * (7 + chips),
        [rhs_buf, dma((size // step_of(size),))],
        6 * size * rank * cols, ANY,
    )


def solution(mesh):
    placed = (
        P(("leaf", "wide"), None),
        P(("leaf", "wide"), None),
        P(("leaf", "wide")),
        P(("leaf", "wide"), None),
        P(("leaf", "wide"), None, None),
        P("wide", "leaf", None),
        P(),
        P(),
        P(("leaf", "wide"), None),
        P(("leaf", "wide")),
    )
    return jax.shard_map(shards, mesh=mesh, in_specs=placed, out_specs=P(("leaf", "wide"), None), check_vma=False)
```

```python
import functools
import math

import jax
import jax.numpy as jnp
from jax import lax
from jax.experimental import pallas as pl
from jax.experimental.pallas import tpu as pltpu
from jax.sharding import PartitionSpec as P

BF = jnp.bfloat16
F32 = jnp.float32
VMEM_BYTES = 28 << 20


def halves(x):
    hi = x.astype(BF)
    return hi, (x - hi.astype(F32)).astype(BF)


def expand(x, second):
    features = x.shape[1]
    hi, lo = halves(x * F32(math.sqrt(4.0 / features * math.log2(math.e))))
    hi_wide = hi.astype(F32)
    norm = jnp.sum(hi_wide * (hi_wide * 0.5 + lo.astype(F32)), axis=1, keepdims=True) * -1.0
    a = norm.astype(BF).astype(F32)
    b = (norm - a).astype(BF).astype(F32)
    c = norm - a - b
    lane = lax.broadcasted_iota(jnp.int32, x.shape, 1)
    k = 3 if second else 0
    ones = jnp.where(lane < 6, F32(1.0), F32(0.0))
    ext = jnp.where(lane == k, a, jnp.where(lane == k + 1, b, jnp.where(lane == k + 2, c, ones))).astype(BF)
    return jnp.concatenate([hi, hi, lo, ext] if second else [hi, lo, hi, ext], axis=1)


def dot(left, right):
    return lax.dot_general(left, right, (((1,), (0,)), ((), ())), preferred_element_type=F32)


def dot_last(left, right):
    return lax.dot_general(left, right, (((1,), (1,)), ((), ())), preferred_element_type=F32)


def dot_first(left, right):
    return lax.dot_general(left, right, (((0,), (0,)), ((), ())), preferred_element_type=F32)


def product(left, right, op=dot):
    lh, ll = halves(left)
    rh, rl = halves(right)
    return op(lh, rh) + op(ll, rh) + op(lh, rl)


def tile_product(targets, sources, value_hi, value_lo, step):
    total = None
    for start in range(0, sources.shape[0], step):
        span = pl.ds(start, step)
        hi, lo = halves(jnp.exp2(dot_last(targets, sources[span, :])))
        part = dot(hi, value_hi[span, :]) + dot(lo, value_hi[span, :]) + dot(hi, value_lo[span, :])
        total = part if total is None else total + part
    return total


def step_of(count):
    return 256 if count % 256 == 0 else count


def near_flag(near_ids, near_count, offset):
    wide = lax.axis_size("wide")
    wanted = lax.axis_index("leaf") * wide + lax.axis_index("wide") + offset
    found = jnp.int32(0)
    for slot in range(near_ids.shape[1]):
        hit = (near_ids[0, slot] == wanted) & (slot < near_count[0])
        found = found | hit.astype(jnp.int32)
    return found > 0


def hot_rows(order_ref):
    n = order_ref.shape[1]
    row = lax.broadcasted_iota(jnp.int32, (n, n), 0)
    return jnp.where(row == order_ref[...], F32(1.0), F32(0.0)).astype(BF)


def fetch(pairs, sems):
    copies = [pltpu.make_async_copy(src, dst, sems.at[k]) for k, (src, dst) in enumerate(pairs)]
    for copy in copies:
        copy.start()
    return copies


def front_kernel(order_hbm, x_hbm, w_hbm, v_hbm, t_hbm, s_hbm, spots_ref, rows_ref, sum_ref, va_ref, vb_ref, order_ref, x, w, v, t, s, sems):
    first, *copies = fetch(
        ((order_hbm, order_ref), (x_hbm, x), (w_hbm, w), (v_hbm, v), (t_hbm, t), (s_hbm, s)), sems
    )
    first.wait()
    hot = hot_rows(order_ref)
    width = x.shape[1]
    copies[0].wait()
    hi, lo = halves(x[...])
    both = dot(hot, jnp.concatenate([hi, lo], axis=1))
    spots_ref[...] = both[:, :width] + both[:, width:]
    copies[1].wait()
    hi, lo = halves(w[...])
    rows = dot(hot, hi)
    rows_lo = dot(hot, lo)
    rows_ref[...] = rows + rows_lo
    rh, rl = rows.astype(BF), rows_lo.astype(BF)
    copies[2].wait()
    half = va_ref.shape[0]
    va_ref[...] = v[:half, :]
    vb_ref[...] = v[half:, :]
    vh, vl = halves(v[...])
    coef = dot_first(rh, vh) + dot_first(rl, vh) + dot_first(rh, vl)
    copies[3].wait()
    copies[4].wait()
    rank = t.shape[1]
    sum_ref[:rank, :] = product(t[0], coef, dot_first)
    sum_ref[rank:, : s.shape[2]] = s[0]
    sum_ref[rank:, s.shape[2] :] = s[0]


def chip_kernel(own_ref, mate_ref, keep_ref, *send_refs):
    leaf = lax.axis_index("leaf")
    chips = len(send_refs) + 1
    features = (keep_ref.shape[1] - own_ref.shape[1]) // 2
    cols = own_ref.shape[1]
    block = keep_ref.shape[0]
    rank = own_ref.shape[0] - block
    for shift, ref in enumerate((keep_ref,) + send_refs):
        chip = lax.rem(leaf // 2 + shift, chips)
        span = pl.ds(pl.multiple_of((2 * chip + leaf % 2) * block, block), block)
        ref[:, :cols] = own_ref[span, :] + mate_ref[span, :]
        ref[:, cols : cols + features] = own_ref[rank:, :features]
        ref[:, cols + features :] = mate_ref[rank:, :features]


def gather_kernel(*refs):
    received, (block_ref, skel_ref) = refs[:-2], refs[-2:]
    leaf = lax.axis_index("leaf")
    chips = len(received)
    features = skel_ref.shape[1]
    cols = block_ref.shape[1] - features
    block = block_ref.shape[0]
    total = received[0][:, :cols]
    for ref in received[1:]:
        total = total + ref[:, :cols]
    block_ref[:, :cols] = total
    block_ref[:, cols:] = received[0][:, cols : cols + features]
    core = leaf % 2
    for shift, ref in enumerate(received):
        chip = lax.rem(leaf // 2 - shift + chips, chips)
        same = pl.multiple_of((2 * chip + core) * block, block)
        mate = pl.multiple_of((2 * chip + 1 - core) * block, block)
        skel_ref[pl.ds(same, block), :] = ref[:, cols : cols + features]
        skel_ref[pl.ds(mate, block), :] = ref[:, cols + features :]


def pair_kernel(block_ref, other_ref, o_ref):
    even = lax.axis_index("wide") % 2 == 0
    o_ref[0] = jnp.where(even, block_ref[...], other_ref[...])
    o_ref[1] = jnp.where(even, other_ref[...], block_ref[...])


def self_kernel(x_ref, v_hbm, o_ref, v, wide, vh, vl, sems):
    copies = fetch(((v_hbm, v),), sems)
    x = x_ref[...]
    wide[...] = expand(x, True)
    targets = expand(x, False)
    copies[0].wait()
    vh[...], vl[...] = halves(v[...])
    o_ref[...] = tile_product(targets, wide, vh, vl, step_of(v.shape[0]))


def is_heavy():
    return (lax.axis_index("wide") + lax.axis_index("leaf")) % 2 == 0


def sides():
    partner = 1 - 2 * (lax.axis_index("wide") % 2)
    return partner, -partner


def pair_product_kernel(heavy, a_ref, b_ref, *refs):
    v_refs, (o_ref, wide, vh, vl) = refs[:-4], refs[-4:]

    @pl.when(is_heavy() == heavy)
    def _():
        wide[...] = expand(b_ref[...], True)
        targets = expand(a_ref[...], False)
        start = 0
        for ref in v_refs:
            span = pl.ds(start, ref.shape[0])
            vh[span, :], vl[span, :] = halves(ref[...])
            start += ref.shape[0]
        o_ref[...] = tile_product(targets, wide, vh, vl, step_of(vh.shape[0]))


def far_kernel(pairs, ids_hbm, count_hbm, skel_ref, *refs):
    block_refs, (o_ref, wide, vh, vl, ids_ref, count_ref, sems) = refs[:pairs], refs[pairs:]
    copies = fetch(((ids_hbm, ids_ref), (count_hbm, count_ref)), sems)
    cols = o_ref.shape[1]
    rows = block_refs[0].shape[1]
    me = lax.axis_index("wide")
    pair = me // 2
    for k in range(pairs):
        for side in range(2):
            wide[pl.ds((2 * k + side) * rows, rows), :] = expand(block_refs[k][side, :, cols:], True)
    targets = expand(skel_ref[...], False)
    for copy in copies:
        copy.wait()
    for k in range(pairs):
        for side in range(2):
            other = 2 * lax.rem(pair - k + pairs, pairs) + side
            wanted = jnp.int32(0)
            for slot in range(ids_ref.shape[1]):
                hit = (ids_ref[me, slot] == other) & (slot < count_ref[me])
                wanted = wanted | hit.astype(jnp.int32)
            span = pl.ds((2 * k + side) * rows, rows)
            hi, lo = halves(jnp.where(wanted > 0, block_refs[k][side, :, :cols], F32(0.0)))
            vh[span, :] = hi
            vl[span, :] = lo
    o_ref[...] = tile_product(targets, wide, vh, vl, step_of(2 * pairs * rows))


def add_kernel(a_ref, b_ref, o_ref):
    o_ref[...] = a_ref[...] + b_ref[...]


def last_kernel(chips, ids_ref, count_ref, total, rows, t, near_ref, far_ref, own_ref, mine_ref, *refs):
    field_refs, (kept_ref, o_hbm, out, sems) = refs[:chips], refs[chips:]
    heavy = is_heavy()
    partner, other = sides()
    to_partner = near_flag(ids_ref, count_ref, partner)
    to_other = near_flag(ids_ref, count_ref, other)
    field = kept_ref[...]
    for ref in field_refs:
        field = field + ref[...]
    lh, ll = halves(product(t[0], field))
    step = step_of(out.shape[0])
    stores = []
    for k in range(out.shape[0] // step):
        span = pl.ds(k * step, step)
        rh, rl = halves(rows[span, :])
        block = total[span, :] + dot(rh, lh) + dot(rl, lh) + dot(rh, ll)
        first = jnp.where(heavy, mine_ref[span, :], near_ref[span, :])
        second = jnp.where(heavy, own_ref[span, :], far_ref[span, :])
        block = block + jnp.where(to_partner, first, F32(0.0))
        out[span, :] = block + jnp.where(to_other, second, F32(0.0))
        stores.append(pltpu.make_async_copy(out.at[span, :], o_hbm.at[span, :], sems.at[k]))
        stores[-1].start()
    for store in stores:
        store.wait()


VM = pl.BlockSpec(memory_space=pltpu.VMEM)
SM = pl.BlockSpec(memory_space=pltpu.SMEM)
ANY = pl.BlockSpec(memory_space=pl.ANY)
HBM = pl.BlockSpec(memory_space=pltpu.HBM)


def kernel_call(body, out, args, specs, scratch=(), flops=0, out_spec=VM):
    many = isinstance(out[0], tuple)
    outs = out if many else (out,)
    moved = 4 * (sum(a.size for a in args) + sum(math.prod(o) for o in outs))
    shapes = tuple(jax.ShapeDtypeStruct(s, F32) for s in outs)
    return pl.pallas_call(
        body,
        out_shape=shapes if many else shapes[0],
        in_specs=specs,
        out_specs=tuple(out_spec for _ in outs) if many else out_spec,
        scratch_shapes=list(scratch),
        compiler_params=pltpu.CompilerParams(vmem_limit_bytes=VMEM_BYTES),
        cost_estimate=pl.CostEstimate(flops=flops, bytes_accessed=moved, transcendentals=0),
    )(*args)


def sent(block, route):
    return lax.ppermute(block, ("leaf", "wide"), route)


def routes(leaf, wide):
    swap, onward, back, back_far, back_next = [], [], [], [], []
    for l in range(leaf):
        step = -2 if l % 2 else 2
        for p in range(wide):
            here, mate, partner = l * wide + p, (l ^ 1) * wide + p, l * wide + (p ^ 1)
            if (l + p) % 2:
                swap.append((here, partner))
                continue
            back.append((here, partner))
            if 0 <= p + step < wide:
                swap.append((here + step, mate))
                onward.append((here, mate))
                back_far.append((mate, partner))
                back_next.append((mate, here + step))
    return swap, onward, back, back_far, back_next


def shards(rhs, points, order, basis, transfer, skeleton, far_ids, far_count, near_ids, near_count):
    wide = lax.axis_size("wide")
    leaf = lax.axis_size("leaf")
    chips = leaf // 2
    size, cols = rhs.shape
    features = points.shape[1]
    rank = transfer.shape[1]
    rows = rank // leaf
    order = order.reshape(1, size)
    swap, onward, back, back_far, back_next = routes(leaf, wide)
    all_wide = lambda move: [(l * wide + p, move(l, p)) for l in range(leaf) for p in range(wide)]
    mates = all_wide(lambda l, p: (l ^ 1) * wide + p)
    partners = all_wide(lambda l, p: l * wide + (p ^ 1))
    tile_flops = 2 * size * size * (4 * features + 3 * cols)
    dma = pltpu.SemaphoreType.DMA
    spot_buf, rhs_buf = pltpu.VMEM((size, features), F32), pltpu.VMEM((size, cols), F32)
    scratch = [pltpu.VMEM((size, 4 * features), BF), pltpu.VMEM((size, cols), BF), pltpu.VMEM((size, cols), BF)]

    def across_chips(blocks):
        return [
            sent(block, all_wide(lambda l, p: ((l // 2 + shift) % chips * 2 + l % 2) * wide + p))
            for shift, block in enumerate(blocks, 1)
        ]

    def pair_product(heavy, a, b, *v):
        return kernel_call(
            functools.partial(pair_product_kernel, heavy), (size, cols), (a, b) + v, [VM] * (2 + len(v)),
            scratch, tile_flops,
        )

    half = size // 2
    spots, basis_rows, term, rhs_a, rhs_b = kernel_call(
        front_kernel, ((size, features), (size, rank), (rank + rows, cols), (half, cols), (size - half, cols)),
        tuple(pltpu.with_memory_space_constraint(t, pltpu.HBM) for t in (order, points, basis, rhs, transfer, skeleton)),
        [HBM] * 6,
        [pltpu.VMEM((1, size), jnp.int32), spot_buf, pltpu.VMEM((size, rank), F32), rhs_buf, pltpu.VMEM(transfer.shape, F32), pltpu.VMEM(skeleton.shape, F32), dma((6,))],
        4 * size * size * (rank + features),
    )
    mate_term = sent(term, mates)
    spots_in = sent(spots, swap)
    kept, *sends = kernel_call(chip_kernel, ((rows, cols + 2 * features),) * chips, (term, mate_term), [VM] * 2)
    received = across_chips(sends)
    total = kernel_call(self_kernel, (size, cols), (spots, rhs), [VM, ANY], [rhs_buf] + scratch + [dma((1,))], tile_flops)
    block, skel = kernel_call(
        gather_kernel, ((rows, cols + features), (rank, features)), (kept, *received), [VM] * chips
    )
    other = sent(block, partners)
    rhs_in = (sent(rhs_a, swap), sent(rhs_b, swap))
    spots_far = sent(spots_in, onward)
    pair = kernel_call(pair_kernel, (2,) + block.shape, (block, other), [VM] * 2)
    pairs = [pair] + [sent(pair, all_wide(lambda l, p: l * wide + (p + 2 * k) % wide)) for k in range(1, wide // 2)]
    share_near = sent(pair_product(True, spots_in, spots, rhs), back)
    share_far = sent(pair_product(False, spots_far, spots_in, *rhs_in), back_far)
    rhs_far = (sent(rhs_in[0], onward), sent(rhs_in[1], onward))
    mine = pair_product(True, spots, spots_in, *rhs_in)
    field = kernel_call(
        functools.partial(far_kernel, len(pairs)), (rank, cols),
        (pltpu.with_memory_space_constraint(far_ids, pltpu.HBM), pltpu.with_memory_space_constraint(far_count, pltpu.HBM), skel, *pairs),
        [HBM, HBM] + [VM] * (1 + len(pairs)),
        [pltpu.VMEM((wide * rows, 4 * features), BF), pltpu.VMEM((wide * rows, cols), BF), pltpu.VMEM((wide * rows, cols), BF)]
        + [pltpu.SMEM(far_ids.shape, jnp.int32), pltpu.SMEM(far_count.shape, jnp.int32), dma((2,))],
        2 * rank * rows * wide * (4 * features + 3 * cols),
    )
    mate_field = sent(field, mates)
    field = kernel_call(add_kernel, (rank, cols), (field, mate_field), [VM] * 2)
    fields = across_chips([field] * (chips - 1))
    own_far = sent(pair_product(False, spots_in, spots_far, *rhs_far), back_next)
    return kernel_call(
        functools.partial(last_kernel, chips - 1), (size, cols),
        (near_ids, near_count, total, basis_rows, transfer, share_near, share_far, own_far, mine, *fields, field),
        [SM, SM] + [VM] * (7 + chips),
        [rhs_buf, dma((size // step_of(size),))],
        6 * size * rank * cols, ANY,
    )


def solution(mesh):
    placed = (
        P(("leaf", "wide"), None),
        P(("leaf", "wide"), None),
        P(("leaf", "wide")),
        P(("leaf", "wide"), None),
        P(("leaf", "wide"), None, None),
        P("wide", "leaf", None),
        P(),
        P(),
        P(("leaf", "wide"), None),
        P(("leaf", "wide")),
    )
    return jax.shard_map(shards, mesh=mesh, in_specs=placed, out_specs=P(("leaf", "wide"), None), check_vma=False)
```

```python
import functools
import math

import jax
import jax.numpy as jnp
from jax import lax
from jax.experimental import pallas as pl
from jax.experimental.pallas import tpu as pltpu
from jax.sharding import PartitionSpec as P

BF = jnp.bfloat16
F32 = jnp.float32
VMEM_BYTES = 28 << 20


def halves(x):
    hi = x.astype(BF)
    return hi, (x - hi.astype(F32)).astype(BF)


def expand(x, second):
    features = x.shape[1]
    hi, lo = halves(x * F32(math.sqrt(4.0 / features * math.log2(math.e))))
    hi_wide = hi.astype(F32)
    norm = jnp.sum(hi_wide * (hi_wide * 0.5 + lo.astype(F32)), axis=1, keepdims=True) * -1.0
    a = norm.astype(BF).astype(F32)
    b = (norm - a).astype(BF).astype(F32)
    c = norm - a - b
    lane = lax.broadcasted_iota(jnp.int32, x.shape, 1)
    k = 3 if second else 0
    ones = jnp.where(lane < 6, F32(1.0), F32(0.0))
    ext = jnp.where(lane == k, a, jnp.where(lane == k + 1, b, jnp.where(lane == k + 2, c, ones))).astype(BF)
    return jnp.concatenate([hi, hi, lo, ext] if second else [hi, lo, hi, ext], axis=1)


def dot(left, right):
    return lax.dot_general(left, right, (((1,), (0,)), ((), ())), preferred_element_type=F32)


def dot_last(left, right):
    return lax.dot_general(left, right, (((1,), (1,)), ((), ())), preferred_element_type=F32)


def dot_first(left, right):
    return lax.dot_general(left, right, (((0,), (0,)), ((), ())), preferred_element_type=F32)


def product(left, right, op=dot):
    lh, ll = halves(left)
    rh, rl = halves(right)
    return op(lh, rh) + op(ll, rh) + op(lh, rl)


def tile_product(targets, sources, value_hi, value_lo, step):
    total = None
    for start in range(0, sources.shape[0], step):
        span = pl.ds(start, step)
        hi, lo = halves(jnp.exp2(dot_last(targets, sources[span, :])))
        part = dot(hi, value_hi[span, :]) + dot(lo, value_hi[span, :]) + dot(hi, value_lo[span, :])
        total = part if total is None else total + part
    return total


def step_of(count):
    return 256 if count % 256 == 0 else count


def near_flag(near_ids, near_count, offset):
    wide = lax.axis_size("wide")
    wanted = lax.axis_index("leaf") * wide + lax.axis_index("wide") + offset
    found = jnp.int32(0)
    for slot in range(near_ids.shape[1]):
        hit = (near_ids[0, slot] == wanted) & (slot < near_count[0])
        found = found | hit.astype(jnp.int32)
    return found > 0


def hot_rows(order_ref):
    n = order_ref.shape[1]
    row = lax.broadcasted_iota(jnp.int32, (n, n), 0)
    return jnp.where(row == order_ref[...], F32(1.0), F32(0.0)).astype(BF)


def fetch(pairs, sems):
    copies = [pltpu.make_async_copy(src, dst, sems.at[k]) for k, (src, dst) in enumerate(pairs)]
    for copy in copies:
        copy.start()
    return copies


def front_kernel(order_hbm, x_hbm, w_hbm, v_hbm, t_hbm, s_hbm, spots_ref, rows_ref, sum_ref, va_ref, vb_ref, order_ref, x, w, v, t, s, sems):
    first, *copies = fetch(
        ((order_hbm, order_ref), (x_hbm, x), (w_hbm, w), (v_hbm, v), (t_hbm, t), (s_hbm, s)), sems
    )
    first.wait()
    hot = hot_rows(order_ref)
    width = x.shape[1]
    copies[0].wait()
    hi, lo = halves(x[...])
    both = dot(hot, jnp.concatenate([hi, lo], axis=1))
    spots_ref[...] = both[:, :width] + both[:, width:]
    copies[1].wait()
    hi, lo = halves(w[...])
    rows = dot(hot, hi)
    rows_lo = dot(hot, lo)
    rows_ref[...] = rows + rows_lo
    rh, rl = rows.astype(BF), rows_lo.astype(BF)
    copies[2].wait()
    half = va_ref.shape[0]
    va_ref[...] = v[:half, :]
    vb_ref[...] = v[half:, :]
    vh, vl = halves(v[...])
    coef = dot_first(rh, vh) + dot_first(rl, vh) + dot_first(rh, vl)
    copies[3].wait()
    copies[4].wait()
    rank = t.shape[1]
    sum_ref[:rank, :] = product(t[0], coef, dot_first)
    sum_ref[rank:, : s.shape[2]] = s[0]
    sum_ref[rank:, s.shape[2] :] = s[0]


def chip_kernel(own_ref, mate_ref, next_ref, mate_next_ref, keep_ref, *send_refs):
    leaf = lax.axis_index("leaf")
    chips = len(send_refs) + 1
    features = next_ref.shape[1]
    cols = own_ref.shape[1]
    block = keep_ref.shape[0]
    rank = own_ref.shape[0] - block
    skels = own_ref[rank:, :features], mate_ref[rank:, :features], next_ref[...], mate_next_ref[...]
    for shift, ref in enumerate((keep_ref,) + send_refs):
        chip = lax.rem(leaf // 2 + shift, chips)
        span = pl.ds(pl.multiple_of((2 * chip + leaf % 2) * block, block), block)
        ref[:, :cols] = own_ref[span, :] + mate_ref[span, :]
        for k, skel in enumerate(skels):
            ref[:, cols + k * features : cols + (k + 1) * features] = skel


def gather_kernel(*refs):
    received, (block_ref, skel_ref) = refs[:-2], refs[-2:]
    leaf = lax.axis_index("leaf")
    chips = len(received)
    features = skel_ref.shape[2]
    cols = block_ref.shape[1] - features
    block = block_ref.shape[0]
    total = received[0][:, :cols]
    for ref in received[1:]:
        total = total + ref[:, :cols]
    block_ref[:, :cols] = total
    block_ref[:, cols:] = received[0][:, cols : cols + features]
    core = leaf % 2
    for shift, ref in enumerate(received):
        chip = lax.rem(leaf // 2 - shift + chips, chips)
        for k, place in enumerate((core, 1 - core, core, 1 - core)):
            span = pl.ds(pl.multiple_of((2 * chip + place) * block, block), block)
            skel_ref[k // 2, span, :] = ref[:, cols + k * features : cols + (k + 1) * features]


def self_kernel(x_ref, v_hbm, o_ref, v, wide, vh, vl, sems):
    copies = fetch(((v_hbm, v),), sems)
    x = x_ref[...]
    wide[...] = expand(x, True)
    targets = expand(x, False)
    copies[0].wait()
    vh[...], vl[...] = halves(v[...])
    o_ref[...] = tile_product(targets, wide, vh, vl, step_of(v.shape[0]))


def is_heavy():
    return (lax.axis_index("wide") + lax.axis_index("leaf")) % 2 == 0


def sides():
    partner = 1 - 2 * (lax.axis_index("wide") % 2)
    return partner, -partner


def pair_product_kernel(heavy, a_ref, b_ref, *refs):
    v_refs, (o_ref, wide, vh, vl) = refs[:-4], refs[-4:]

    @pl.when(is_heavy() == heavy)
    def _():
        wide[...] = expand(b_ref[...], True)
        targets = expand(a_ref[...], False)
        start = 0
        for ref in v_refs:
            span = pl.ds(start, ref.shape[0])
            vh[span, :], vl[span, :] = halves(ref[...])
            start += ref.shape[0]
        o_ref[...] = tile_product(targets, wide, vh, vl, step_of(vh.shape[0]))


def far_kernel(count, ids_hbm, count_hbm, skel_ref, *refs):
    block_refs, (keep_ref, give_ref, wide, vh, vl, ids_ref, count_ref, sems) = refs[:count], refs[count:]
    copies = fetch(((ids_hbm, ids_ref), (count_hbm, count_ref)), sems)
    cols = keep_ref.shape[1]
    rows = block_refs[0].shape[0]
    parents = lax.axis_size("wide")
    me = lax.axis_index("wide")
    spans = [pl.ds(k * rows, rows) for k in range(count)]
    for k, span in enumerate(spans):
        wide[span, :] = expand(block_refs[k][:, cols:], True)
    for copy in copies:
        copy.wait()
    heavy = is_heavy()
    for ref, kept in ((keep_ref, True), (give_ref, False)):
        index = jnp.where(heavy == kept, 0, 1)
        target = jnp.where(index == 0, me, me + 1 - 2 * (me % 2))
        for k, span in enumerate(spans):
            other = lax.rem(me - 2 * k + parents, parents)
            wanted = jnp.int32(0)
            for slot in range(ids_ref.shape[1]):
                hit = (ids_ref[target, slot] == other) & (slot < count_ref[target])
                wanted = wanted | hit.astype(jnp.int32)
            vh[span, :], vl[span, :] = halves(jnp.where(wanted > 0, block_refs[k][:, :cols], F32(0.0)))
        ref[...] = tile_product(expand(skel_ref[index], False), wide, vh, vl, step_of(count * rows))


def add_kernel(*refs):
    total = refs[0][...]
    for ref in refs[1:-1]:
        total = total + ref[...]
    refs[-1][...] = total


def last_kernel(ids_ref, count_ref, total, rows, t, near_ref, far_ref, own_ref, mine_ref, kept_ref, mate_ref, o_hbm, out, sems):
    heavy = is_heavy()
    partner, other = sides()
    to_partner = near_flag(ids_ref, count_ref, partner)
    to_other = near_flag(ids_ref, count_ref, other)
    field = jnp.where(heavy, kept_ref[...], mate_ref[...])
    lh, ll = halves(product(t[0], field))
    step = step_of(out.shape[0])
    stores = []
    for k in range(out.shape[0] // step):
        span = pl.ds(k * step, step)
        rh, rl = halves(rows[span, :])
        block = total[span, :] + dot(rh, lh) + dot(rl, lh) + dot(rh, ll)
        first = jnp.where(heavy, mine_ref[span, :], near_ref[span, :])
        second = jnp.where(heavy, own_ref[span, :], far_ref[span, :])
        block = block + jnp.where(to_partner, first, F32(0.0))
        out[span, :] = block + jnp.where(to_other, second, F32(0.0))
        stores.append(pltpu.make_async_copy(out.at[span, :], o_hbm.at[span, :], sems.at[k]))
        stores[-1].start()
    for store in stores:
        store.wait()


VM = pl.BlockSpec(memory_space=pltpu.VMEM)
SM = pl.BlockSpec(memory_space=pltpu.SMEM)
ANY = pl.BlockSpec(memory_space=pl.ANY)
HBM = pl.BlockSpec(memory_space=pltpu.HBM)


def kernel_call(body, out, args, specs, scratch=(), flops=0, out_spec=VM):
    many = isinstance(out[0], tuple)
    outs = out if many else (out,)
    moved = 4 * (sum(a.size for a in args) + sum(math.prod(o) for o in outs))
    shapes = tuple(jax.ShapeDtypeStruct(s, F32) for s in outs)
    return pl.pallas_call(
        body,
        out_shape=shapes if many else shapes[0],
        in_specs=specs,
        out_specs=tuple(out_spec for _ in outs) if many else out_spec,
        scratch_shapes=list(scratch),
        compiler_params=pltpu.CompilerParams(vmem_limit_bytes=VMEM_BYTES),
        cost_estimate=pl.CostEstimate(flops=flops, bytes_accessed=moved, transcendentals=0),
    )(*args)


def sent(block, route):
    return lax.ppermute(block, ("leaf", "wide"), route)


def routes(leaf, wide):
    swap, onward, back, back_far, to_mate = [], [], [], [], []
    for l in range(leaf):
        step = -2 if l % 2 else 2
        for p in range(wide):
            here, mate, partner = l * wide + p, (l ^ 1) * wide + p, l * wide + (p ^ 1)
            if (l + p) % 2:
                swap.append((here, partner))
                continue
            swap.append((here, mate))
            back.append((here, partner))
            to_mate.append((mate, here))
            if 0 <= p + step < wide:
                onward.append((here, mate + step))
            if 0 <= p - step // 2 < wide:
                back_far.append((mate, here - step // 2))
    return swap, onward, back, back_far, to_mate


def shards(rhs, points, order, basis, transfer, skeleton, far_ids, far_count, near_ids, near_count):
    wide = lax.axis_size("wide")
    leaf = lax.axis_size("leaf")
    chips = leaf // 2
    size, cols = rhs.shape
    features = points.shape[1]
    rank = transfer.shape[1]
    rows = rank // leaf
    order = order.reshape(1, size)
    swap, onward, back, back_far, to_mate = routes(leaf, wide)
    all_wide = lambda move: [(l * wide + p, move(l, p)) for l in range(leaf) for p in range(wide)]
    mates = all_wide(lambda l, p: (l ^ 1) * wide + p)
    partners = all_wide(lambda l, p: l * wide + (p ^ 1))
    tile_flops = 2 * size * size * (4 * features + 3 * cols)
    dma = pltpu.SemaphoreType.DMA
    spot_buf, rhs_buf = pltpu.VMEM((size, features), F32), pltpu.VMEM((size, cols), F32)
    scratch = [pltpu.VMEM((size, 4 * features), BF), pltpu.VMEM((size, cols), BF), pltpu.VMEM((size, cols), BF)]

    def across_chips(blocks, senders):
        moves = [all_wide(lambda l, p: ((l // 2 + shift) % chips * 2 + l % 2) * wide + p) for shift in range(1, chips)]
        return [sent(block, [pair for pair in move if pair[0] in senders]) for block, move in zip(blocks, moves)]

    def pair_product(heavy, a, b, *v):
        return kernel_call(
            functools.partial(pair_product_kernel, heavy), (size, cols), (a, b) + v, [VM] * (2 + len(v)),
            scratch, tile_flops,
        )

    half = size // 2
    skel_next = sent(skeleton[0], partners)
    spots, basis_rows, term, rhs_a, rhs_b = kernel_call(
        front_kernel, ((size, features), (size, rank), (rank + rows, cols), (half, cols), (size - half, cols)),
        tuple(pltpu.with_memory_space_constraint(t, pltpu.HBM) for t in (order, points, basis, rhs, transfer, skeleton)),
        [HBM] * 6,
        [pltpu.VMEM((1, size), jnp.int32), spot_buf, pltpu.VMEM((size, rank), F32), rhs_buf, pltpu.VMEM(transfer.shape, F32), pltpu.VMEM(skeleton.shape, F32), dma((6,))],
        4 * size * size * (rank + features),
    )
    mate_term = sent(term, mates)
    spots_in = sent(spots, swap)
    mate_next = sent(skel_next, mates)
    kept, *sends = kernel_call(
        chip_kernel, ((rows, cols + 4 * features),) * chips, (term, mate_term, skel_next, mate_next), [VM] * 4
    )
    received = across_chips(sends, range(leaf * wide))
    total = kernel_call(self_kernel, (size, cols), (spots, rhs), [VM, ANY], [rhs_buf] + scratch + [dma((1,))], tile_flops)
    block, skel = kernel_call(
        gather_kernel, ((rows, cols + features), (2, rank, features)), (kept, *received), [VM] * chips
    )
    rhs_in = (sent(rhs_a, swap), sent(rhs_b, swap))
    spots_far = sent(spots_in, onward)
    blocks = [block] + [sent(block, all_wide(lambda l, p: l * wide + (p + 2 * k) % wide)) for k in range(1, wide // 2)]
    share_near = sent(pair_product(True, spots_in, spots, rhs), back)
    share_far = sent(pair_product(False, spots_far, spots_in, *rhs_in), back_far)
    rhs_far = (sent(rhs_in[0], onward), sent(rhs_in[1], onward))
    mine = pair_product(True, spots, spots_in, *rhs_in)
    sources = len(blocks) * rows
    keep, give = kernel_call(
        functools.partial(far_kernel, len(blocks)), ((rank, cols),) * 2,
        (pltpu.with_memory_space_constraint(far_ids, pltpu.HBM), pltpu.with_memory_space_constraint(far_count, pltpu.HBM), skel, *blocks),
        [HBM, HBM] + [VM] * (1 + len(blocks)),
        [pltpu.VMEM((sources, 4 * features), BF), pltpu.VMEM((sources, cols), BF), pltpu.VMEM((sources, cols), BF)]
        + [pltpu.SMEM(far_ids.shape, jnp.int32), pltpu.SMEM(far_count.shape, jnp.int32), dma((2,))],
        4 * rank * sources * (4 * features + 3 * cols),
    )

    def added(*terms):
        return kernel_call(add_kernel, (rank, cols), terms, [VM] * len(terms))

    heavies = [here for here, _ in back]
    keep = added(keep, sent(give, mates))
    keep = added(keep, sent(keep, [(there, here) for here, there in back]))
    fields = across_chips([keep] * (chips - 1), heavies)
    field = added(keep, *fields)
    mate_field = sent(field, [(here, mate) for here, mate in mates if here in heavies])
    own_far = sent(pair_product(False, spots_in, spots_far, *rhs_far), to_mate)
    return kernel_call(
        last_kernel, (size, cols),
        (near_ids, near_count, total, basis_rows, transfer, share_near, share_far, own_far, mine, field, mate_field),
        [SM, SM] + [VM] * 9,
        [rhs_buf, dma((size // step_of(size),))],
        6 * size * rank * cols, ANY,
    )


def solution(mesh):
    placed = (
        P(("leaf", "wide"), None),
        P(("leaf", "wide"), None),
        P(("leaf", "wide")),
        P(("leaf", "wide"), None),
        P(("leaf", "wide"), None, None),
        P("wide", "leaf", None),
        P(),
        P(),
        P(("leaf", "wide"), None),
        P(("leaf", "wide")),
    )
    return jax.shard_map(shards, mesh=mesh, in_specs=placed, out_specs=P(("leaf", "wide"), None), check_vma=False)
```

```python
import functools
import math

import jax
import jax.numpy as jnp
from jax import lax
from jax.experimental import pallas as pl
from jax.experimental.pallas import tpu as pltpu
from jax.sharding import PartitionSpec as P

BF = jnp.bfloat16
F32 = jnp.float32
VMEM_BYTES = 28 << 20


def halves(x):
    hi = x.astype(BF)
    return hi, (x - hi.astype(F32)).astype(BF)


def expand(x, second):
    features = x.shape[1]
    hi, lo = halves(x * F32(math.sqrt(4.0 / features * math.log2(math.e))))
    hi_wide = hi.astype(F32)
    norm = jnp.sum(hi_wide * (hi_wide * 0.5 + lo.astype(F32)), axis=1, keepdims=True) * -1.0
    a = norm.astype(BF).astype(F32)
    b = (norm - a).astype(BF).astype(F32)
    c = norm - a - b
    lane = lax.broadcasted_iota(jnp.int32, x.shape, 1)
    k = 3 if second else 0
    ones = jnp.where(lane < 6, F32(1.0), F32(0.0))
    ext = jnp.where(lane == k, a, jnp.where(lane == k + 1, b, jnp.where(lane == k + 2, c, ones))).astype(BF)
    return jnp.concatenate([hi, hi, lo, ext] if second else [hi, lo, hi, ext], axis=1)


def dot(left, right):
    return lax.dot_general(left, right, (((1,), (0,)), ((), ())), preferred_element_type=F32)


def dot_last(left, right):
    return lax.dot_general(left, right, (((1,), (1,)), ((), ())), preferred_element_type=F32)


def dot_first(left, right):
    return lax.dot_general(left, right, (((0,), (0,)), ((), ())), preferred_element_type=F32)


def product(left, right, op=dot):
    lh, ll = halves(left)
    rh, rl = halves(right)
    return op(lh, rh) + op(ll, rh) + op(lh, rl)


def tile_product(targets, sources, value_hi, value_lo, step):
    total = None
    for start in range(0, sources.shape[0], step):
        span = pl.ds(start, step)
        hi, lo = halves(jnp.exp2(dot_last(targets, sources[span, :])))
        part = dot(hi, value_hi[span, :]) + dot(lo, value_hi[span, :]) + dot(hi, value_lo[span, :])
        total = part if total is None else total + part
    return total


def step_of(count):
    return 256 if count % 256 == 0 else count


def near_flag(near_ids, near_count, offset):
    wide = lax.axis_size("wide")
    wanted = lax.axis_index("leaf") * wide + lax.axis_index("wide") + offset
    found = jnp.int32(0)
    for slot in range(near_ids.shape[1]):
        hit = (near_ids[0, slot] == wanted) & (slot < near_count[0])
        found = found | hit.astype(jnp.int32)
    return found > 0


def hot_rows(order_ref):
    n = order_ref.shape[1]
    row = lax.broadcasted_iota(jnp.int32, (n, n), 0)
    return jnp.where(row == order_ref[...], F32(1.0), F32(0.0)).astype(BF)


def fetch(pairs, sems):
    copies = [pltpu.make_async_copy(src, dst, sems.at[k]) for k, (src, dst) in enumerate(pairs)]
    for copy in copies:
        copy.start()
    return copies


def front_kernel(order_hbm, x_hbm, w_hbm, v_hbm, t_hbm, s_hbm, spots_ref, rows_ref, sum_ref, va_ref, vb_ref, order_ref, x, w, v, t, s, sems):
    first, *copies = fetch(
        ((order_hbm, order_ref), (x_hbm, x), (w_hbm, w), (v_hbm, v), (t_hbm, t), (s_hbm, s)), sems
    )
    first.wait()
    hot = hot_rows(order_ref)
    width = x.shape[1]
    copies[0].wait()
    hi, lo = halves(x[...])
    both = dot(hot, jnp.concatenate([hi, lo], axis=1))
    spots_ref[...] = both[:, :width] + both[:, width:]
    copies[1].wait()
    hi, lo = halves(w[...])
    rows = dot(hot, hi)
    rows_lo = dot(hot, lo)
    rows_ref[...] = rows + rows_lo
    rh, rl = rows.astype(BF), rows_lo.astype(BF)
    copies[2].wait()
    half = va_ref.shape[0]
    va_ref[...] = v[:half, :]
    vb_ref[...] = v[half:, :]
    vh, vl = halves(v[...])
    coef = dot_first(rh, vh) + dot_first(rl, vh) + dot_first(rh, vl)
    copies[3].wait()
    copies[4].wait()
    rank = t.shape[1]
    sum_ref[:rank, :] = product(t[0], coef, dot_first)
    sum_ref[rank:, : s.shape[2]] = s[0]
    sum_ref[rank:, s.shape[2] :] = s[0]


def chip_kernel(own_ref, mate_ref, keep_ref, *send_refs):
    leaf = lax.axis_index("leaf")
    chips = len(send_refs) + 1
    features = (keep_ref.shape[1] - own_ref.shape[1]) // 2
    cols = own_ref.shape[1]
    block = keep_ref.shape[0]
    rank = own_ref.shape[0] - block
    for shift, ref in enumerate((keep_ref,) + send_refs):
        chip = lax.rem(leaf // 2 + shift, chips)
        span = pl.ds(pl.multiple_of((2 * chip + leaf % 2) * block, block), block)
        ref[:, :cols] = own_ref[span, :] + mate_ref[span, :]
        ref[:, cols : cols + features] = own_ref[rank:, :features]
        ref[:, cols + features :] = mate_ref[rank:, :features]


def gather_kernel(*refs):
    received, (block_ref, skel_ref) = refs[:-2], refs[-2:]
    leaf = lax.axis_index("leaf")
    chips = len(received)
    features = skel_ref.shape[1]
    cols = block_ref.shape[1] - features
    block = block_ref.shape[0]
    total = received[0][:, :cols]
    for ref in received[1:]:
        total = total + ref[:, :cols]
    block_ref[:, :cols] = total
    block_ref[:, cols:] = received[0][:, cols : cols + features]
    core = leaf % 2
    for shift, ref in enumerate(received):
        chip = lax.rem(leaf // 2 - shift + chips, chips)
        same = pl.multiple_of((2 * chip + core) * block, block)
        mate = pl.multiple_of((2 * chip + 1 - core) * block, block)
        skel_ref[pl.ds(same, block), :] = ref[:, cols : cols + features]
        skel_ref[pl.ds(mate, block), :] = ref[:, cols + features :]


def self_kernel(x_ref, v_hbm, o_ref, v, wide, vh, vl, sems):
    copies = fetch(((v_hbm, v),), sems)
    x = x_ref[...]
    wide[...] = expand(x, True)
    targets = expand(x, False)
    copies[0].wait()
    vh[...], vl[...] = halves(v[...])
    o_ref[...] = tile_product(targets, wide, vh, vl, step_of(v.shape[0]))


def is_heavy():
    return (lax.axis_index("wide") + lax.axis_index("leaf")) % 2 == 0


def sides():
    partner = 1 - 2 * (lax.axis_index("wide") % 2)
    return partner, -partner


def pair_product_kernel(heavy, a_ref, b_ref, *refs):
    v_refs, (o_ref, wide, vh, vl) = refs[:-4], refs[-4:]

    @pl.when(is_heavy() == heavy)
    def _():
        wide[...] = expand(b_ref[...], True)
        targets = expand(a_ref[...], False)
        start = 0
        for ref in v_refs:
            span = pl.ds(start, ref.shape[0])
            vh[span, :], vl[span, :] = halves(ref[...])
            start += ref.shape[0]
        o_ref[...] = tile_product(targets, wide, vh, vl, step_of(vh.shape[0]))


def far_kernel(count, ids_hbm, count_hbm, skel_ref, light_skel_ref, heavy_skel_ref, *refs):
    block_refs, (keep_ref, give_ref, wide, vh, vl, ids_ref, count_ref, sems) = refs[:count], refs[count:]
    copies = fetch(((ids_hbm, ids_ref), (count_hbm, count_ref)), sems)
    cols = keep_ref.shape[1]
    rows = block_refs[0].shape[0]
    parents = lax.axis_size("wide")
    me = lax.axis_index("wide")
    spans = [pl.ds(k * rows, rows) for k in range(count)]
    for k, span in enumerate(spans):
        wide[span, :] = expand(block_refs[k][:, cols:], True)
    for copy in copies:
        copy.wait()
    heavy = is_heavy()
    partner_skel = jnp.where(heavy, heavy_skel_ref[...], light_skel_ref[...])
    for ref, kept in ((keep_ref, True), (give_ref, False)):
        own = heavy == kept
        target = jnp.where(own, me, me + 1 - 2 * (me % 2))
        skel = jnp.where(own, skel_ref[...], partner_skel)
        for k, span in enumerate(spans):
            other = lax.rem(me - 2 * k + parents, parents)
            wanted = jnp.int32(0)
            for slot in range(ids_ref.shape[1]):
                hit = (ids_ref[target, slot] == other) & (slot < count_ref[target])
                wanted = wanted | hit.astype(jnp.int32)
            vh[span, :], vl[span, :] = halves(jnp.where(wanted > 0, block_refs[k][:, :cols], F32(0.0)))
        ref[...] = tile_product(expand(skel, False), wide, vh, vl, step_of(count * rows))


def add_kernel(*refs):
    total = refs[0][...]
    for ref in refs[1:-1]:
        total = total + ref[...]
    refs[-1][...] = total


def last_kernel(ids_ref, count_ref, total, rows, t, near_ref, far_ref, own_ref, mine_ref, kept_ref, mate_ref, o_hbm, out, sems):
    heavy = is_heavy()
    partner, other = sides()
    to_partner = near_flag(ids_ref, count_ref, partner)
    to_other = near_flag(ids_ref, count_ref, other)
    field = jnp.where(heavy, kept_ref[...], mate_ref[...])
    lh, ll = halves(product(t[0], field))
    step = step_of(out.shape[0])
    stores = []
    for k in range(out.shape[0] // step):
        span = pl.ds(k * step, step)
        rh, rl = halves(rows[span, :])
        block = total[span, :] + dot(rh, lh) + dot(rl, lh) + dot(rh, ll)
        first = jnp.where(heavy, mine_ref[span, :], near_ref[span, :])
        second = jnp.where(heavy, own_ref[span, :], far_ref[span, :])
        block = block + jnp.where(to_partner, first, F32(0.0))
        out[span, :] = block + jnp.where(to_other, second, F32(0.0))
        stores.append(pltpu.make_async_copy(out.at[span, :], o_hbm.at[span, :], sems.at[k]))
        stores[-1].start()
    for store in stores:
        store.wait()


VM = pl.BlockSpec(memory_space=pltpu.VMEM)
SM = pl.BlockSpec(memory_space=pltpu.SMEM)
ANY = pl.BlockSpec(memory_space=pl.ANY)
HBM = pl.BlockSpec(memory_space=pltpu.HBM)


def kernel_call(body, out, args, specs, scratch=(), flops=0, out_spec=VM):
    many = isinstance(out[0], tuple)
    outs = out if many else (out,)
    moved = 4 * (sum(a.size for a in args) + sum(math.prod(o) for o in outs))
    shapes = tuple(jax.ShapeDtypeStruct(s, F32) for s in outs)
    return pl.pallas_call(
        body,
        out_shape=shapes if many else shapes[0],
        in_specs=specs,
        out_specs=tuple(out_spec for _ in outs) if many else out_spec,
        scratch_shapes=list(scratch),
        compiler_params=pltpu.CompilerParams(vmem_limit_bytes=VMEM_BYTES),
        cost_estimate=pl.CostEstimate(flops=flops, bytes_accessed=moved, transcendentals=0),
    )(*args)


def sent(block, route):
    return lax.ppermute(block, ("leaf", "wide"), route)


def routes(leaf, wide):
    swap, onward, back, back_far, to_mate = [], [], [], [], []
    for l in range(leaf):
        step = -2 if l % 2 else 2
        for p in range(wide):
            here, mate, partner = l * wide + p, (l ^ 1) * wide + p, l * wide + (p ^ 1)
            if (l + p) % 2:
                swap.append((here, partner))
                continue
            swap.append((here, mate))
            back.append((here, partner))
            to_mate.append((mate, here))
            if 0 <= p + step < wide:
                onward.append((here, mate + step))
            if 0 <= p - step // 2 < wide:
                back_far.append((mate, here - step // 2))
    return swap, onward, back, back_far, to_mate


def shards(rhs, points, order, basis, transfer, skeleton, far_ids, far_count, near_ids, near_count):
    wide = lax.axis_size("wide")
    leaf = lax.axis_size("leaf")
    chips = leaf // 2
    size, cols = rhs.shape
    features = points.shape[1]
    rank = transfer.shape[1]
    rows = rank // leaf
    order = order.reshape(1, size)
    swap, onward, back, back_far, to_mate = routes(leaf, wide)
    all_wide = lambda move: [(l * wide + p, move(l, p)) for l in range(leaf) for p in range(wide)]
    mates = all_wide(lambda l, p: (l ^ 1) * wide + p)
    heavies = [here for here, _ in back]
    tile_flops = 2 * size * size * (4 * features + 3 * cols)
    dma = pltpu.SemaphoreType.DMA
    spot_buf, rhs_buf = pltpu.VMEM((size, features), F32), pltpu.VMEM((size, cols), F32)
    scratch = [pltpu.VMEM((size, 4 * features), BF), pltpu.VMEM((size, cols), BF), pltpu.VMEM((size, cols), BF)]

    def across_chips(blocks, senders):
        moves = [all_wide(lambda l, p: ((l // 2 + shift) % chips * 2 + l % 2) * wide + p) for shift in range(1, chips)]
        return [sent(block, [pair for pair in move if pair[0] in senders]) for block, move in zip(blocks, moves)]

    def pair_product(heavy, a, b, *v):
        return kernel_call(
            functools.partial(pair_product_kernel, heavy), (size, cols), (a, b) + v, [VM] * (2 + len(v)),
            scratch, tile_flops,
        )

    half = size // 2
    spots, basis_rows, term, rhs_a, rhs_b = kernel_call(
        front_kernel, ((size, features), (size, rank), (rank + rows, cols), (half, cols), (size - half, cols)),
        tuple(pltpu.with_memory_space_constraint(t, pltpu.HBM) for t in (order, points, basis, rhs, transfer, skeleton)),
        [HBM] * 6,
        [pltpu.VMEM((1, size), jnp.int32), spot_buf, pltpu.VMEM((size, rank), F32), rhs_buf, pltpu.VMEM(transfer.shape, F32), pltpu.VMEM(skeleton.shape, F32), dma((6,))],
        4 * size * size * (rank + features),
    )
    mate_term = sent(term, mates)
    spots_in = sent(spots, swap)
    kept, *sends = kernel_call(chip_kernel, ((rows, cols + 2 * features),) * chips, (term, mate_term), [VM] * 2)
    received = across_chips(sends, range(leaf * wide))
    total = kernel_call(self_kernel, (size, cols), (spots, rhs), [VM, ANY], [rhs_buf] + scratch + [dma((1,))], tile_flops)
    block, skel = kernel_call(
        gather_kernel, ((rows, cols + features), (rank, features)), (kept, *received), [VM] * chips
    )
    light_skel = sent(skel, back)
    heavy_skel = sent(light_skel, [(mate, here) for here, mate in mates if here in heavies])
    rhs_in = (sent(rhs_a, swap), sent(rhs_b, swap))
    spots_far = sent(spots_in, onward)
    blocks = [block] + [sent(block, all_wide(lambda l, p: l * wide + (p + 2 * k) % wide)) for k in range(1, wide // 2)]
    share_near = sent(pair_product(True, spots_in, spots, rhs), back)
    share_far = sent(pair_product(False, spots_far, spots_in, *rhs_in), back_far)
    rhs_far = (sent(rhs_in[0], onward), sent(rhs_in[1], onward))
    mine = pair_product(True, spots, spots_in, *rhs_in)
    sources = len(blocks) * rows
    keep, give = kernel_call(
        functools.partial(far_kernel, len(blocks)), ((rank, cols),) * 2,
        (pltpu.with_memory_space_constraint(far_ids, pltpu.HBM), pltpu.with_memory_space_constraint(far_count, pltpu.HBM), skel, light_skel, heavy_skel, *blocks),
        [HBM, HBM] + [VM] * (3 + len(blocks)),
        [pltpu.VMEM((sources, 4 * features), BF), pltpu.VMEM((sources, cols), BF), pltpu.VMEM((sources, cols), BF)]
        + [pltpu.SMEM(far_ids.shape, jnp.int32), pltpu.SMEM(far_count.shape, jnp.int32), dma((2,))],
        4 * rank * sources * (4 * features + 3 * cols),
    )

    def added(*terms):
        return kernel_call(add_kernel, (rank, cols), terms, [VM] * len(terms))

    keep = added(keep, sent(give, mates))
    keep = added(keep, sent(keep, [(there, here) for here, there in back]))
    fields = across_chips([keep] * (chips - 1), heavies)
    field = added(keep, *fields)
    mate_field = sent(field, [(here, mate) for here, mate in mates if here in heavies])
    own_far = sent(pair_product(False, spots_in, spots_far, *rhs_far), to_mate)
    return kernel_call(
        last_kernel, (size, cols),
        (near_ids, near_count, total, basis_rows, transfer, share_near, share_far, own_far, mine, field, mate_field),
        [SM, SM] + [VM] * 9,
        [rhs_buf, dma((size // step_of(size),))],
        6 * size * rank * cols, ANY,
    )


def solution(mesh):
    placed = (
        P(("leaf", "wide"), None),
        P(("leaf", "wide"), None),
        P(("leaf", "wide")),
        P(("leaf", "wide"), None),
        P(("leaf", "wide"), None, None),
        P("wide", "leaf", None),
        P(),
        P(),
        P(("leaf", "wide"), None),
        P(("leaf", "wide")),
    )
    return jax.shard_map(shards, mesh=mesh, in_specs=placed, out_specs=P(("leaf", "wide"), None), check_vma=False)
```

```python
import functools
import math

import jax
import jax.numpy as jnp
from jax import lax
from jax.experimental import pallas as pl
from jax.experimental.pallas import tpu as pltpu
from jax.sharding import PartitionSpec as P

BF = jnp.bfloat16
F32 = jnp.float32
VMEM_BYTES = 28 << 20


def halves(x):
    hi = x.astype(BF)
    return hi, (x - hi.astype(F32)).astype(BF)


def expand(x, second):
    features = x.shape[1]
    hi, lo = halves(x * F32(math.sqrt(4.0 / features * math.log2(math.e))))
    hi_wide = hi.astype(F32)
    norm = jnp.sum(hi_wide * (hi_wide * 0.5 + lo.astype(F32)), axis=1, keepdims=True) * -1.0
    a = norm.astype(BF).astype(F32)
    b = (norm - a).astype(BF).astype(F32)
    c = norm - a - b
    lane = lax.broadcasted_iota(jnp.int32, x.shape, 1)
    k = 3 if second else 0
    ones = jnp.where(lane < 6, F32(1.0), F32(0.0))
    ext = jnp.where(lane == k, a, jnp.where(lane == k + 1, b, jnp.where(lane == k + 2, c, ones))).astype(BF)
    return jnp.concatenate([hi, hi, lo, ext] if second else [hi, lo, hi, ext], axis=1)


def dot(left, right):
    return lax.dot_general(left, right, (((1,), (0,)), ((), ())), preferred_element_type=F32)


def dot_last(left, right):
    return lax.dot_general(left, right, (((1,), (1,)), ((), ())), preferred_element_type=F32)


def dot_first(left, right):
    return lax.dot_general(left, right, (((0,), (0,)), ((), ())), preferred_element_type=F32)


def product(left, right, op=dot):
    lh, ll = halves(left)
    rh, rl = halves(right)
    return op(lh, rh) + op(ll, rh) + op(lh, rl)


def tile_product(targets, sources, value_hi, value_lo, step):
    total = None
    for start in range(0, sources.shape[0], step):
        span = pl.ds(start, step)
        hi, lo = halves(jnp.exp2(dot_last(targets, sources[span, :])))
        part = dot(hi, value_hi[span, :]) + dot(lo, value_hi[span, :]) + dot(hi, value_lo[span, :])
        total = part if total is None else total + part
    return total


def step_of(count):
    return 256 if count % 256 == 0 else count


def near_flag(near_ids, near_count, offset):
    wide = lax.axis_size("wide")
    wanted = lax.axis_index("leaf") * wide + lax.axis_index("wide") + offset
    found = jnp.int32(0)
    for slot in range(near_ids.shape[1]):
        hit = (near_ids[0, slot] == wanted) & (slot < near_count[0])
        found = found | hit.astype(jnp.int32)
    return found > 0


def hot_rows(order_ref):
    n = order_ref.shape[1]
    row = lax.broadcasted_iota(jnp.int32, (n, n), 0)
    return jnp.where(row == order_ref[...], F32(1.0), F32(0.0)).astype(BF)


def fetch(pairs, sems):
    copies = [pltpu.make_async_copy(src, dst, sems.at[k]) for k, (src, dst) in enumerate(pairs)]
    for copy in copies:
        copy.start()
    return copies


def front_kernel(order_hbm, x_hbm, w_hbm, v_hbm, t_hbm, s_hbm, spots_ref, rows_ref, sum_ref, va_ref, vb_ref, order_ref, x, w, v, t, s, sems):
    first, *copies = fetch(
        ((order_hbm, order_ref), (x_hbm, x), (w_hbm, w), (v_hbm, v), (t_hbm, t), (s_hbm, s)), sems
    )
    first.wait()
    hot = hot_rows(order_ref)
    width = x.shape[1]
    copies[0].wait()
    hi, lo = halves(x[...])
    both = dot(hot, jnp.concatenate([hi, lo], axis=1))
    spots_ref[...] = both[:, :width] + both[:, width:]
    copies[1].wait()
    hi, lo = halves(w[...])
    rows = dot(hot, hi)
    rows_lo = dot(hot, lo)
    rows_ref[...] = rows + rows_lo
    rh, rl = rows.astype(BF), rows_lo.astype(BF)
    copies[2].wait()
    half = va_ref.shape[0]
    va_ref[...] = v[:half, :]
    vb_ref[...] = v[half:, :]
    vh, vl = halves(v[...])
    coef = dot_first(rh, vh) + dot_first(rl, vh) + dot_first(rh, vl)
    copies[3].wait()
    copies[4].wait()
    rank = t.shape[1]
    sum_ref[:rank, :] = product(t[0], coef, dot_first)
    sum_ref[rank:, : s.shape[2]] = s[0]
    sum_ref[rank:, s.shape[2] :] = s[0]


def is_heavy():
    return (lax.axis_index("wide") + lax.axis_index("leaf")) % 2 == 0


def sides():
    partner = 1 - 2 * (lax.axis_index("wide") % 2)
    return partner, -partner


def light_only(body):
    @functools.wraps(body)
    def kernel(*refs):
        @pl.when(jnp.logical_not(is_heavy()))
        def _():
            body(*refs)

    return kernel


@light_only
def chip_kernel(own_ref, mate_ref, next_ref, mate_next_ref, keep_ref, *send_refs):
    leaf = lax.axis_index("leaf")
    chips = len(send_refs) + 1
    features = next_ref.shape[1]
    cols = own_ref.shape[1]
    block = keep_ref.shape[0]
    half = next_ref.shape[0]
    rank = own_ref.shape[0] - half
    core = leaf % 2
    places = [pl.ds(pl.multiple_of(place * half, half), half) for place in (core, 1 - core)]
    for shift, ref in enumerate((keep_ref,) + send_refs):
        chip = lax.rem(leaf // 2 + shift, chips)
        span = pl.ds(pl.multiple_of(chip * block, block), block)
        ref[:, :cols] = own_ref[span, :] + mate_ref[span, :]
        for place, term, skel in zip(places, (own_ref, mate_ref), (next_ref, mate_next_ref)):
            ref[place, cols : cols + features] = term[rank:, :features]
            ref[place, cols + features :] = skel[...]


@light_only
def gather_kernel(*refs):
    received, (block_ref, skel_ref) = refs[:-2], refs[-2:]
    leaf = lax.axis_index("leaf")
    chips = len(received)
    features = skel_ref.shape[2]
    cols = block_ref.shape[1] - features
    block = block_ref.shape[0]
    total = received[0][:, :cols]
    for ref in received[1:]:
        total = total + ref[:, :cols]
    block_ref[:, :cols] = total
    block_ref[:, cols:] = received[0][:, cols : cols + features]
    for shift, ref in enumerate(received):
        chip = lax.rem(leaf // 2 - shift + chips, chips)
        span = pl.ds(pl.multiple_of(chip * block, block), block)
        for k in range(2):
            skel_ref[k, span, :] = ref[:, cols + k * features : cols + (k + 1) * features]


def self_kernel(x_ref, v_hbm, o_ref, v, wide, vh, vl, sems):
    copies = fetch(((v_hbm, v),), sems)
    x = x_ref[...]
    wide[...] = expand(x, True)
    targets = expand(x, False)
    copies[0].wait()
    vh[...], vl[...] = halves(v[...])
    o_ref[...] = tile_product(targets, wide, vh, vl, step_of(v.shape[0]))


def pair_product_kernel(heavy, a_ref, b_ref, *refs):
    v_refs, (o_ref, wide, vh, vl) = refs[:-4], refs[-4:]

    @pl.when(is_heavy() == heavy)
    def _():
        wide[...] = expand(b_ref[...], True)
        targets = expand(a_ref[...], False)
        start = 0
        for ref in v_refs:
            span = pl.ds(start, ref.shape[0])
            vh[span, :], vl[span, :] = halves(ref[...])
            start += ref.shape[0]
        o_ref[...] = tile_product(targets, wide, vh, vl, step_of(vh.shape[0]))


def far_kernel(count, ids_hbm, count_hbm, skel_ref, *refs):
    block_refs, (keep_ref, give_ref, wide, vh, vl, ids_ref, count_ref, sems) = refs[:count], refs[count:]

    @pl.when(jnp.logical_not(is_heavy()))
    def _():
        copies = fetch(((ids_hbm, ids_ref), (count_hbm, count_ref)), sems)
        cols = keep_ref.shape[1]
        rows = block_refs[0].shape[0]
        parents = lax.axis_size("wide")
        me = lax.axis_index("wide")
        spans = [pl.ds(k * rows, rows) for k in range(count)]
        for k, span in enumerate(spans):
            wide[span, :] = expand(block_refs[k][:, cols:], True)
        for copy in copies:
            copy.wait()
        for index, (ref, target) in enumerate(((keep_ref, me), (give_ref, me + 1 - 2 * (me % 2)))):
            for k, span in enumerate(spans):
                other = lax.rem(me - 2 * k + parents, parents)
                wanted = jnp.int32(0)
                for slot in range(ids_ref.shape[1]):
                    hit = (ids_ref[target, slot] == other) & (slot < count_ref[target])
                    wanted = wanted | hit.astype(jnp.int32)
                vh[span, :], vl[span, :] = halves(jnp.where(wanted > 0, block_refs[k][:, :cols], F32(0.0)))
            ref[...] = tile_product(expand(skel_ref[index], False), wide, vh, vl, step_of(count * rows))


@light_only
def add_kernel(*refs):
    total = refs[0][...]
    for ref in refs[1:-1]:
        total = total + ref[...]
    refs[-1][...] = total


def last_kernel(ids_ref, count_ref, total, rows, t, near_ref, far_ref, own_ref, mine_ref, kept_ref, mate_ref, o_hbm, out, sems):
    heavy = is_heavy()
    partner, other = sides()
    to_partner = near_flag(ids_ref, count_ref, partner)
    to_other = near_flag(ids_ref, count_ref, other)
    field = jnp.where(heavy, mate_ref[...], kept_ref[...])
    lh, ll = halves(product(t[0], field))
    step = step_of(out.shape[0])
    stores = []
    for k in range(out.shape[0] // step):
        span = pl.ds(k * step, step)
        rh, rl = halves(rows[span, :])
        block = total[span, :] + dot(rh, lh) + dot(rl, lh) + dot(rh, ll)
        first = jnp.where(heavy, mine_ref[span, :], near_ref[span, :])
        second = jnp.where(heavy, own_ref[span, :], far_ref[span, :])
        block = block + jnp.where(to_partner, first, F32(0.0))
        out[span, :] = block + jnp.where(to_other, second, F32(0.0))
        stores.append(pltpu.make_async_copy(out.at[span, :], o_hbm.at[span, :], sems.at[k]))
        stores[-1].start()
    for store in stores:
        store.wait()


VM = pl.BlockSpec(memory_space=pltpu.VMEM)
SM = pl.BlockSpec(memory_space=pltpu.SMEM)
ANY = pl.BlockSpec(memory_space=pl.ANY)
HBM = pl.BlockSpec(memory_space=pltpu.HBM)


def kernel_call(body, out, args, specs, scratch=(), flops=0, out_spec=VM):
    many = isinstance(out[0], tuple)
    outs = out if many else (out,)
    moved = 4 * (sum(a.size for a in args) + sum(math.prod(o) for o in outs))
    shapes = tuple(jax.ShapeDtypeStruct(s, F32) for s in outs)
    return pl.pallas_call(
        body,
        out_shape=shapes if many else shapes[0],
        in_specs=specs,
        out_specs=tuple(out_spec for _ in outs) if many else out_spec,
        scratch_shapes=list(scratch),
        compiler_params=pltpu.CompilerParams(vmem_limit_bytes=VMEM_BYTES),
        cost_estimate=pl.CostEstimate(flops=flops, bytes_accessed=moved, transcendentals=0),
    )(*args)


def sent(block, route):
    return lax.ppermute(block, ("leaf", "wide"), route)


def routes(leaf, wide):
    swap, onward, back, back_far, to_mate = [], [], [], [], []
    for l in range(leaf):
        step = -2 if l % 2 else 2
        for p in range(wide):
            here, mate, partner = l * wide + p, (l ^ 1) * wide + p, l * wide + (p ^ 1)
            if (l + p) % 2:
                swap.append((here, partner))
                continue
            swap.append((here, mate))
            back.append((here, partner))
            to_mate.append((mate, here))
            if 0 <= p + step < wide:
                onward.append((here, mate + step))
            if 0 <= p - step // 2 < wide:
                back_far.append((mate, here - step // 2))
    return swap, onward, back, back_far, to_mate


def shards(rhs, points, order, basis, transfer, skeleton, far_ids, far_count, near_ids, near_count):
    wide = lax.axis_size("wide")
    leaf = lax.axis_size("leaf")
    chips = leaf // 2
    size, cols = rhs.shape
    features = points.shape[1]
    rank = transfer.shape[1]
    rows = rank // leaf
    order = order.reshape(1, size)
    swap, onward, back, back_far, to_mate = routes(leaf, wide)
    all_wide = lambda move: [(l * wide + p, move(l, p)) for l in range(leaf) for p in range(wide)]
    lights = [here for here, _ in swap if here not in dict(back)]

    def lights_to(move):
        return [pair for pair in all_wide(move) if pair[0] in lights]

    mates = all_wide(lambda l, p: (l ^ 1) * wide + p)
    partners = all_wide(lambda l, p: l * wide + (p ^ 1))
    tile_flops = 2 * size * size * (4 * features + 3 * cols)
    dma = pltpu.SemaphoreType.DMA
    spot_buf, rhs_buf = pltpu.VMEM((size, features), F32), pltpu.VMEM((size, cols), F32)
    scratch = [pltpu.VMEM((size, 4 * features), BF), pltpu.VMEM((size, cols), BF), pltpu.VMEM((size, cols), BF)]

    def across_chips(blocks, senders):
        moves = [all_wide(lambda l, p: ((l // 2 + shift) % chips * 2 + l % 2) * wide + p) for shift in range(1, chips)]
        return [sent(block, [pair for pair in move if pair[0] in senders]) for block, move in zip(blocks, moves)]

    def pair_product(heavy, a, b, *v):
        return kernel_call(
            functools.partial(pair_product_kernel, heavy), (size, cols), (a, b) + v, [VM] * (2 + len(v)),
            scratch, tile_flops,
        )

    half = size // 2
    skel_next = sent(skeleton[0], partners)
    spots, basis_rows, term, rhs_a, rhs_b = kernel_call(
        front_kernel, ((size, features), (size, rank), (rank + rows, cols), (half, cols), (size - half, cols)),
        tuple(pltpu.with_memory_space_constraint(t, pltpu.HBM) for t in (order, points, basis, rhs, transfer, skeleton)),
        [HBM] * 6,
        [pltpu.VMEM((1, size), jnp.int32), spot_buf, pltpu.VMEM((size, rank), F32), rhs_buf, pltpu.VMEM(transfer.shape, F32), pltpu.VMEM(skeleton.shape, F32), dma((6,))],
        4 * size * size * (rank + features),
    )
    mate_term = sent(term, mates)
    spots_in = sent(spots, swap)
    mate_next = sent(skel_next, mates)
    kept, *sends = kernel_call(
        chip_kernel, ((2 * rows, cols + 2 * features),) * chips, (term, mate_term, skel_next, mate_next), [VM] * 4
    )
    received = across_chips(sends, lights)
    total = kernel_call(self_kernel, (size, cols), (spots, rhs), [VM, ANY], [rhs_buf] + scratch + [dma((1,))], tile_flops)
    block, skel = kernel_call(
        gather_kernel, ((2 * rows, cols + features), (2, rank, features)), (kept, *received), [VM] * chips
    )
    rhs_in = (sent(rhs_a, swap), sent(rhs_b, swap))
    spots_far = sent(spots_in, onward)
    blocks = [block] + [sent(block, lights_to(lambda l, p: l * wide + (p + 2 * k) % wide)) for k in range(1, wide // 2)]
    share_near = sent(pair_product(True, spots_in, spots, rhs), back)
    share_far = sent(pair_product(False, spots_far, spots_in, *rhs_in), back_far)
    rhs_far = (sent(rhs_in[0], onward), sent(rhs_in[1], onward))
    mine = pair_product(True, spots, spots_in, *rhs_in)
    sources = 2 * len(blocks) * rows
    keep, give = kernel_call(
        functools.partial(far_kernel, len(blocks)), ((rank, cols),) * 2,
        (pltpu.with_memory_space_constraint(far_ids, pltpu.HBM), pltpu.with_memory_space_constraint(far_count, pltpu.HBM), skel, *blocks),
        [HBM, HBM] + [VM] * (1 + len(blocks)),
        [pltpu.VMEM((sources, 4 * features), BF), pltpu.VMEM((sources, cols), BF), pltpu.VMEM((sources, cols), BF)]
        + [pltpu.SMEM(far_ids.shape, jnp.int32), pltpu.SMEM(far_count.shape, jnp.int32), dma((2,))],
        4 * rank * sources * (4 * features + 3 * cols),
    )

    def added(*terms):
        return kernel_call(add_kernel, (rank, cols), terms, [VM] * len(terms))

    keep = added(keep, sent(give, lights_to(lambda l, p: (l ^ 1) * wide + (p ^ 1))))
    field = added(keep, *across_chips([keep] * (chips - 1), lights))
    mate_field = sent(field, lights_to(lambda l, p: (l ^ 1) * wide + p))
    own_far = sent(pair_product(False, spots_in, spots_far, *rhs_far), to_mate)
    return kernel_call(
        last_kernel, (size, cols),
        (near_ids, near_count, total, basis_rows, transfer, share_near, share_far, own_far, mine, field, mate_field),
        [SM, SM] + [VM] * 9,
        [rhs_buf, dma((size // step_of(size),))],
        6 * size * rank * cols, ANY,
    )


def solution(mesh):
    placed = (
        P(("leaf", "wide"), None),
        P(("leaf", "wide"), None),
        P(("leaf", "wide")),
        P(("leaf", "wide"), None),
        P(("leaf", "wide"), None, None),
        P("wide", "leaf", None),
        P(),
        P(),
        P(("leaf", "wide"), None),
        P(("leaf", "wide")),
    )
    return jax.shard_map(shards, mesh=mesh, in_specs=placed, out_specs=P(("leaf", "wide"), None), check_vma=False)
```

```python
import functools
import math

import jax
import jax.numpy as jnp
from jax import lax
from jax.experimental import pallas as pl
from jax.experimental.pallas import tpu as pltpu
from jax.sharding import PartitionSpec as P

BF = jnp.bfloat16
F32 = jnp.float32
VMEM_BYTES = 28 << 20


def halves(x):
    hi = x.astype(BF)
    return hi, (x - hi.astype(F32)).astype(BF)


def expand(x, second):
    features = x.shape[1]
    hi, lo = halves(x * F32(math.sqrt(4.0 / features * math.log2(math.e))))
    hi_wide = hi.astype(F32)
    norm = jnp.sum(hi_wide * (hi_wide * 0.5 + lo.astype(F32)), axis=1, keepdims=True) * -1.0
    a = norm.astype(BF).astype(F32)
    b = (norm - a).astype(BF).astype(F32)
    c = norm - a - b
    lane = lax.broadcasted_iota(jnp.int32, x.shape, 1)
    k = 3 if second else 0
    ones = jnp.where(lane < 6, F32(1.0), F32(0.0))
    ext = jnp.where(lane == k, a, jnp.where(lane == k + 1, b, jnp.where(lane == k + 2, c, ones))).astype(BF)
    return jnp.concatenate([hi, hi, lo, ext] if second else [hi, lo, hi, ext], axis=1)


def dot(left, right):
    return lax.dot_general(left, right, (((1,), (0,)), ((), ())), preferred_element_type=F32)


def dot_last(left, right):
    return lax.dot_general(left, right, (((1,), (1,)), ((), ())), preferred_element_type=F32)


def dot_first(left, right):
    return lax.dot_general(left, right, (((0,), (0,)), ((), ())), preferred_element_type=F32)


def product(left, right, op=dot):
    lh, ll = halves(left)
    rh, rl = halves(right)
    return op(lh, rh) + op(ll, rh) + op(lh, rl)


def tile_product(targets, sources, value_hi, value_lo, step):
    total = None
    for start in range(0, sources.shape[0], step):
        span = pl.ds(start, step)
        hi, lo = halves(jnp.exp2(dot_last(targets, sources[span, :])))
        part = dot(hi, value_hi[span, :]) + dot(lo, value_hi[span, :]) + dot(hi, value_lo[span, :])
        total = part if total is None else total + part
    return total


def step_of(count):
    return 256 if count % 256 == 0 else count


def near_flag(near_ids, near_count, offset):
    wide = lax.axis_size("wide")
    wanted = lax.axis_index("leaf") * wide + lax.axis_index("wide") + offset
    found = jnp.int32(0)
    for slot in range(near_ids.shape[1]):
        hit = (near_ids[0, slot] == wanted) & (slot < near_count[0])
        found = found | hit.astype(jnp.int32)
    return found > 0


def hot_rows(order_ref):
    n = order_ref.shape[1]
    row = lax.broadcasted_iota(jnp.int32, (n, n), 0)
    return jnp.where(row == order_ref[...], F32(1.0), F32(0.0)).astype(BF)


def fetch(pairs, sems):
    copies = [pltpu.make_async_copy(src, dst, sems.at[k]) for k, (src, dst) in enumerate(pairs)]
    for copy in copies:
        copy.start()
    return copies


def front_kernel(order_hbm, x_hbm, w_hbm, v_hbm, t_hbm, s_hbm, spots_ref, rows_ref, sum_ref, va_ref, vb_ref, order_ref, x, w, v, t, s, sems):
    first, *copies = fetch(
        ((order_hbm, order_ref), (x_hbm, x), (w_hbm, w), (v_hbm, v), (t_hbm, t), (s_hbm, s)), sems
    )
    first.wait()
    hot = hot_rows(order_ref)
    width = x.shape[1]
    copies[0].wait()
    hi, lo = halves(x[...])
    both = dot(hot, jnp.concatenate([hi, lo], axis=1))
    spots_ref[...] = both[:, :width] + both[:, width:]
    copies[1].wait()
    hi, lo = halves(w[...])
    rows = dot(hot, hi)
    rows_lo = dot(hot, lo)
    rows_ref[...] = rows + rows_lo
    rh, rl = rows.astype(BF), rows_lo.astype(BF)
    copies[2].wait()
    half = va_ref.shape[0]
    va_ref[...] = v[:half, :]
    vb_ref[...] = v[half:, :]
    vh, vl = halves(v[...])
    coef = dot_first(rh, vh) + dot_first(rl, vh) + dot_first(rh, vl)
    copies[3].wait()
    copies[4].wait()
    rank = t.shape[1]
    sum_ref[:rank, :] = product(t[0], coef, dot_first)
    sum_ref[rank:, : s.shape[2]] = s[0]
    sum_ref[rank:, s.shape[2] :] = s[0]


def chip_kernel(own_ref, mate_ref, next_ref, mate_next_ref, keep_ref, *send_refs):
    leaf = lax.axis_index("leaf")
    chips = len(send_refs) + 1
    features = next_ref.shape[1]
    cols = own_ref.shape[1]
    block = keep_ref.shape[0]
    rank = own_ref.shape[0] - block
    skels = own_ref[rank:, :features], mate_ref[rank:, :features], next_ref[...], mate_next_ref[...]
    for shift, ref in enumerate((keep_ref,) + send_refs):
        chip = lax.rem(leaf // 2 + shift, chips)
        span = pl.ds(pl.multiple_of((2 * chip + leaf % 2) * block, block), block)
        ref[:, :cols] = own_ref[span, :] + mate_ref[span, :]
        for k, skel in enumerate(skels):
            ref[:, cols + k * features : cols + (k + 1) * features] = skel


def gather_kernel(*refs):
    received, (block_ref, skel_ref) = refs[:-2], refs[-2:]
    leaf = lax.axis_index("leaf")
    chips = len(received)
    features = skel_ref.shape[2]
    cols = block_ref.shape[1] - features
    block = block_ref.shape[0]
    total = received[0][:, :cols]
    for ref in received[1:]:
        total = total + ref[:, :cols]
    block_ref[:, :cols] = total
    block_ref[:, cols:] = received[0][:, cols : cols + features]
    core = leaf % 2
    for shift, ref in enumerate(received):
        chip = lax.rem(leaf // 2 - shift + chips, chips)
        for k, place in enumerate((core, 1 - core, core, 1 - core)):
            span = pl.ds(pl.multiple_of((2 * chip + place) * block, block), block)
            skel_ref[k // 2, span, :] = ref[:, cols + k * features : cols + (k + 1) * features]


def self_kernel(x_ref, v_hbm, o_ref, v, wide, vh, vl, sems):
    copies = fetch(((v_hbm, v),), sems)
    x = x_ref[...]
    wide[...] = expand(x, True)
    targets = expand(x, False)
    copies[0].wait()
    vh[...], vl[...] = halves(v[...])
    o_ref[...] = tile_product(targets, wide, vh, vl, step_of(v.shape[0]))


def is_heavy():
    return (lax.axis_index("wide") + lax.axis_index("leaf")) % 2 == 0


def sides():
    partner = 1 - 2 * (lax.axis_index("wide") % 2)
    return partner, -partner


def pair_product_kernel(heavy, a_ref, b_ref, *refs):
    v_refs, (o_ref, wide, vh, vl) = refs[:-4], refs[-4:]

    @pl.when(is_heavy() == heavy)
    def _():
        wide[...] = expand(b_ref[...], True)
        targets = expand(a_ref[...], False)
        start = 0
        for ref in v_refs:
            span = pl.ds(start, ref.shape[0])
            vh[span, :], vl[span, :] = halves(ref[...])
            start += ref.shape[0]
        o_ref[...] = tile_product(targets, wide, vh, vl, step_of(vh.shape[0]))


def far_kernel(count, ids_hbm, count_hbm, skel_ref, *refs):
    block_refs, (keep_ref, give_ref, wide, vh, vl, ids_ref, count_ref, sems) = refs[:count], refs[count:]
    copies = fetch(((ids_hbm, ids_ref), (count_hbm, count_ref)), sems)
    cols = keep_ref.shape[1]
    rows = block_refs[0].shape[0]
    parents = lax.axis_size("wide")
    me = lax.axis_index("wide")
    spans = [pl.ds(k * rows, rows) for k in range(count)]
    for k, span in enumerate(spans):
        wide[span, :] = expand(block_refs[k][:, cols:], True)
    for copy in copies:
        copy.wait()
    heavy = is_heavy()
    for ref, kept in ((keep_ref, True), (give_ref, False)):
        index = jnp.where(heavy == kept, 0, 1)
        target = jnp.where(index == 0, me, me + 1 - 2 * (me % 2))
        for k, span in enumerate(spans):
            other = lax.rem(me - 2 * k + parents, parents)
            wanted = jnp.int32(0)
            for slot in range(ids_ref.shape[1]):
                hit = (ids_ref[target, slot] == other) & (slot < count_ref[target])
                wanted = wanted | hit.astype(jnp.int32)
            vh[span, :], vl[span, :] = halves(jnp.where(wanted > 0, block_refs[k][:, :cols], F32(0.0)))
        ref[...] = tile_product(expand(skel_ref[index], False), wide, vh, vl, step_of(count * rows))


def add_kernel(*refs):
    total = refs[0][...]
    for ref in refs[1:-1]:
        total = total + ref[...]
    refs[-1][...] = total


def lower_kernel(total_ref, rows_ref, t_ref, kept_ref, mate_ref, o_ref):
    field = jnp.where(is_heavy(), kept_ref[...], mate_ref[...])
    o_ref[...] = total_ref[...] + product(rows_ref[...], product(t_ref[0], field))


def last_kernel(ids_ref, count_ref, total_ref, near_ref, far_ref, own_ref, mine_ref, o_hbm, out, sems):
    heavy = is_heavy()
    partner, other = sides()
    to_partner = near_flag(ids_ref, count_ref, partner)
    to_other = near_flag(ids_ref, count_ref, other)
    step = out.shape[0] // 8
    spans = [pl.ds(k * step, step) for k in range(out.shape[0] // step)]
    stores = [pltpu.make_async_copy(out.at[span, :], o_hbm.at[span, :], sems.at[k]) for k, span in enumerate(spans)]

    def put(first_ref, second_ref):
        for span, store in zip(spans, stores):
            block = total_ref[span, :] + jnp.where(to_partner, first_ref[span, :], F32(0.0))
            out[span, :] = block + jnp.where(to_other, second_ref[span, :], F32(0.0))
            store.start()
        for store in stores:
            store.wait()

    @pl.when(heavy)
    def _():
        put(mine_ref, own_ref)

    @pl.when(jnp.logical_not(heavy))
    def _():
        put(near_ref, far_ref)


VM = pl.BlockSpec(memory_space=pltpu.VMEM)
SM = pl.BlockSpec(memory_space=pltpu.SMEM)
ANY = pl.BlockSpec(memory_space=pl.ANY)
HBM = pl.BlockSpec(memory_space=pltpu.HBM)


def kernel_call(body, out, args, specs, scratch=(), flops=0, out_spec=VM):
    many = isinstance(out[0], tuple)
    outs = out if many else (out,)
    moved = 4 * (sum(a.size for a in args) + sum(math.prod(o) for o in outs))
    shapes = tuple(jax.ShapeDtypeStruct(s, F32) for s in outs)
    return pl.pallas_call(
        body,
        out_shape=shapes if many else shapes[0],
        in_specs=specs,
        out_specs=tuple(out_spec for _ in outs) if many else out_spec,
        scratch_shapes=list(scratch),
        compiler_params=pltpu.CompilerParams(vmem_limit_bytes=VMEM_BYTES),
        cost_estimate=pl.CostEstimate(flops=flops, bytes_accessed=moved, transcendentals=0),
    )(*args)


def sent(block, route):
    return lax.ppermute(block, ("leaf", "wide"), route)


def routes(leaf, wide):
    swap, onward, back, back_far, to_mate = [], [], [], [], []
    for l in range(leaf):
        step = -2 if l % 2 else 2
        for p in range(wide):
            here, mate, partner = l * wide + p, (l ^ 1) * wide + p, l * wide + (p ^ 1)
            if (l + p) % 2:
                swap.append((here, partner))
                continue
            swap.append((here, mate))
            back.append((here, partner))
            to_mate.append((mate, here))
            if 0 <= p + step < wide:
                onward.append((here, mate + step))
            if 0 <= p - step // 2 < wide:
                back_far.append((mate, here - step // 2))
    return swap, onward, back, back_far, to_mate


def shards(rhs, points, order, basis, transfer, skeleton, far_ids, far_count, near_ids, near_count):
    wide = lax.axis_size("wide")
    leaf = lax.axis_size("leaf")
    chips = leaf // 2
    size, cols = rhs.shape
    features = points.shape[1]
    rank = transfer.shape[1]
    rows = rank // leaf
    order = order.reshape(1, size)
    swap, onward, back, back_far, to_mate = routes(leaf, wide)
    all_wide = lambda move: [(l * wide + p, move(l, p)) for l in range(leaf) for p in range(wide)]
    mates = all_wide(lambda l, p: (l ^ 1) * wide + p)
    partners = all_wide(lambda l, p: l * wide + (p ^ 1))
    tile_flops = 2 * size * size * (4 * features + 3 * cols)
    dma = pltpu.SemaphoreType.DMA
    spot_buf, rhs_buf = pltpu.VMEM((size, features), F32), pltpu.VMEM((size, cols), F32)
    scratch = [pltpu.VMEM((size, 4 * features), BF), pltpu.VMEM((size, cols), BF), pltpu.VMEM((size, cols), BF)]

    def across_chips(blocks, senders):
        moves = [all_wide(lambda l, p: ((l // 2 + shift) % chips * 2 + l % 2) * wide + p) for shift in range(1, chips)]
        return [sent(block, [pair for pair in move if pair[0] in senders]) for block, move in zip(blocks, moves)]

    def pair_product(heavy, a, b, *v):
        return kernel_call(
            functools.partial(pair_product_kernel, heavy), (size, cols), (a, b) + v, [VM] * (2 + len(v)),
            scratch, tile_flops,
        )

    half = size // 2
    skel_next = sent(skeleton[0], partners)
    spots, basis_rows, term, rhs_a, rhs_b = kernel_call(
        front_kernel, ((size, features), (size, rank), (rank + rows, cols), (half, cols), (size - half, cols)),
        tuple(pltpu.with_memory_space_constraint(t, pltpu.HBM) for t in (order, points, basis, rhs, transfer, skeleton)),
        [HBM] * 6,
        [pltpu.VMEM((1, size), jnp.int32), spot_buf, pltpu.VMEM((size, rank), F32), rhs_buf, pltpu.VMEM(transfer.shape, F32), pltpu.VMEM(skeleton.shape, F32), dma((6,))],
        4 * size * size * (rank + features),
    )
    mate_term = sent(term, mates)
    spots_in = sent(spots, swap)
    mate_next = sent(skel_next, mates)
    kept, *sends = kernel_call(
        chip_kernel, ((rows, cols + 4 * features),) * chips, (term, mate_term, skel_next, mate_next), [VM] * 4
    )
    received = across_chips(sends, range(leaf * wide))
    total = kernel_call(self_kernel, (size, cols), (spots, rhs), [VM, ANY], [rhs_buf] + scratch + [dma((1,))], tile_flops)
    block, skel = kernel_call(
        gather_kernel, ((rows, cols + features), (2, rank, features)), (kept, *received), [VM] * chips
    )
    rhs_in = (sent(rhs_a, swap), sent(rhs_b, swap))
    spots_far = sent(spots_in, onward)
    blocks = [block] + [sent(block, all_wide(lambda l, p: l * wide + (p + 2 * k) % wide)) for k in range(1, wide // 2)]
    share_near = sent(pair_product(True, spots_in, spots, rhs), back)
    share_far = sent(pair_product(False, spots_far, spots_in, *rhs_in), back_far)
    rhs_far = (sent(rhs_in[0], onward), sent(rhs_in[1], onward))
    mine = pair_product(True, spots, spots_in, *rhs_in)
    sources = len(blocks) * rows
    keep, give = kernel_call(
        functools.partial(far_kernel, len(blocks)), ((rank, cols),) * 2,
        (pltpu.with_memory_space_constraint(far_ids, pltpu.HBM), pltpu.with_memory_space_constraint(far_count, pltpu.HBM), skel, *blocks),
        [HBM, HBM] + [VM] * (1 + len(blocks)),
        [pltpu.VMEM((sources, 4 * features), BF), pltpu.VMEM((sources, cols), BF), pltpu.VMEM((sources, cols), BF)]
        + [pltpu.SMEM(far_ids.shape, jnp.int32), pltpu.SMEM(far_count.shape, jnp.int32), dma((2,))],
        4 * rank * sources * (4 * features + 3 * cols),
    )

    def added(*terms):
        return kernel_call(add_kernel, (rank, cols), terms, [VM] * len(terms))

    heavies = [here for here, _ in back]
    keep = added(keep, sent(give, mates))
    keep = added(keep, sent(keep, [(there, here) for here, there in back]))
    fields = across_chips([keep] * (chips - 1), heavies)
    field = added(keep, *fields)
    mate_field = sent(field, [(here, mate) for here, mate in mates if here in heavies])
    own_far = sent(pair_product(False, spots_in, spots_far, *rhs_far), to_mate)
    total = kernel_call(
        lower_kernel, (size, cols), (total, basis_rows, transfer, field, mate_field), [VM] * 5, (),
        6 * size * rank * cols,
    )
    return kernel_call(
        last_kernel, (size, cols), (near_ids, near_count, total, share_near, share_far, own_far, mine),
        [SM, SM] + [VM] * 5, [rhs_buf, dma((8,))], size * cols, ANY,
    )


def solution(mesh):
    placed = (
        P(("leaf", "wide"), None),
        P(("leaf", "wide"), None),
        P(("leaf", "wide")),
        P(("leaf", "wide"), None),
        P(("leaf", "wide"), None, None),
        P("wide", "leaf", None),
        P(),
        P(),
        P(("leaf", "wide"), None),
        P(("leaf", "wide")),
    )
    return jax.shard_map(shards, mesh=mesh, in_specs=placed, out_specs=P(("leaf", "wide"), None), check_vma=False)
```

```python
import functools
import math

import jax
import jax.numpy as jnp
from jax import lax
from jax.experimental import pallas as pl
from jax.experimental.pallas import tpu as pltpu
from jax.sharding import PartitionSpec as P

BF = jnp.bfloat16
F32 = jnp.float32
VMEM_BYTES = 28 << 20


def halves(x):
    hi = x.astype(BF)
    return hi, (x - hi.astype(F32)).astype(BF)


def expand(x, second):
    features = x.shape[1]
    hi, lo = halves(x * F32(math.sqrt(4.0 / features * math.log2(math.e))))
    hi_wide = hi.astype(F32)
    norm = jnp.sum(hi_wide * (hi_wide * 0.5 + lo.astype(F32)), axis=1, keepdims=True) * -1.0
    a = norm.astype(BF).astype(F32)
    b = (norm - a).astype(BF).astype(F32)
    c = norm - a - b
    lane = lax.broadcasted_iota(jnp.int32, x.shape, 1)
    k = 3 if second else 0
    ones = jnp.where(lane < 6, F32(1.0), F32(0.0))
    ext = jnp.where(lane == k, a, jnp.where(lane == k + 1, b, jnp.where(lane == k + 2, c, ones))).astype(BF)
    return jnp.concatenate([hi, hi, lo, ext] if second else [hi, lo, hi, ext], axis=1)


def dot(left, right):
    return lax.dot_general(left, right, (((1,), (0,)), ((), ())), preferred_element_type=F32)


def dot_last(left, right):
    return lax.dot_general(left, right, (((1,), (1,)), ((), ())), preferred_element_type=F32)


def dot_first(left, right):
    return lax.dot_general(left, right, (((0,), (0,)), ((), ())), preferred_element_type=F32)


def product(left, right, op=dot):
    lh, ll = halves(left)
    rh, rl = halves(right)
    return op(lh, rh) + op(ll, rh) + op(lh, rl)


def tile_product(targets, sources, value_hi, value_lo, step):
    total = None
    for start in range(0, sources.shape[0], step):
        span = pl.ds(start, step)
        hi, lo = halves(jnp.exp2(dot_last(targets, sources[span, :])))
        part = dot(hi, value_hi[span, :]) + dot(lo, value_hi[span, :]) + dot(hi, value_lo[span, :])
        total = part if total is None else total + part
    return total


def step_of(count):
    return 256 if count % 256 == 0 else count


def near_flag(near_ids, near_count, offset):
    wide = lax.axis_size("wide")
    wanted = lax.axis_index("leaf") * wide + lax.axis_index("wide") + offset
    found = jnp.int32(0)
    for slot in range(near_ids.shape[1]):
        hit = (near_ids[0, slot] == wanted) & (slot < near_count[0])
        found = found | hit.astype(jnp.int32)
    return found > 0


def hot_rows(order_ref):
    n = order_ref.shape[1]
    row = lax.broadcasted_iota(jnp.int32, (n, n), 0)
    return jnp.where(row == order_ref[...], F32(1.0), F32(0.0)).astype(BF)


def fetch(pairs, sems):
    copies = [pltpu.make_async_copy(src, dst, sems.at[k]) for k, (src, dst) in enumerate(pairs)]
    for copy in copies:
        copy.start()
    return copies


def first_kernel(v_hbm, o_ref, sems):
    copy = pltpu.make_async_copy(v_hbm.at[pl.ds(0, o_ref.shape[0]), :], o_ref, sems.at[0])
    copy.start()
    copy.wait()


def front_kernel(order_hbm, x_hbm, w_hbm, v_hbm, t_hbm, spots_ref, rows_ref, sum_ref, vb_ref, order_ref, x, w, v, t, sems):
    first, *copies = fetch(
        ((order_hbm, order_ref), (x_hbm, x), (w_hbm, w), (v_hbm, v), (t_hbm, t)), sems
    )
    first.wait()
    hot = hot_rows(order_ref)
    width = x.shape[1]
    copies[0].wait()
    hi, lo = halves(x[...])
    both = dot(hot, jnp.concatenate([hi, lo], axis=1))
    spots_ref[...] = both[:, :width] + both[:, width:]
    copies[1].wait()
    hi, lo = halves(w[...])
    rows = dot(hot, hi)
    rows_lo = dot(hot, lo)
    rows_ref[...] = rows + rows_lo
    rh, rl = rows.astype(BF), rows_lo.astype(BF)
    copies[2].wait()
    vb_ref[...] = v[v.shape[0] - vb_ref.shape[0] :, :]
    vh, vl = halves(v[...])
    coef = dot_first(rh, vh) + dot_first(rl, vh) + dot_first(rh, vl)
    copies[3].wait()
    sum_ref[...] = product(t[0], coef, dot_first)


def chip_kernel(own_ref, mate_ref, skel_ref, next_ref, keep_ref, *send_refs):
    leaf = lax.axis_index("leaf")
    chips = len(send_refs) + 1
    features = next_ref.shape[1]
    cols = own_ref.shape[1]
    block = keep_ref.shape[0]
    for shift, ref in enumerate((keep_ref,) + send_refs):
        chip = lax.rem(leaf // 2 + shift, chips)
        span = pl.ds(pl.multiple_of((2 * chip + leaf % 2) * block, block), block)
        ref[:, :cols] = own_ref[span, :] + mate_ref[span, :]
        ref[:, cols : cols + features] = skel_ref[0]
        ref[:, cols + features :] = next_ref[...]


def gather_kernel(*refs):
    received, (block_ref, skels_ref) = refs[:-2], refs[-2:]
    leaf = lax.axis_index("leaf")
    chips = len(received)
    features = skels_ref.shape[2]
    cols = block_ref.shape[1] - features
    block = block_ref.shape[0]
    total = received[0][:, :cols]
    for ref in received[1:]:
        total = total + ref[:, :cols]
    block_ref[:, :cols] = total
    block_ref[:, cols:] = received[0][:, cols : cols + features]
    for shift, ref in enumerate(received):
        chip = lax.rem(leaf // 2 - shift + chips, chips)
        span = pl.ds(pl.multiple_of(chip * block, block), block)
        for k in range(2):
            skels_ref[k, span, :] = ref[:, cols + k * features : cols + (k + 1) * features]


def self_kernel(x_ref, v_hbm, o_ref, v, wide, vh, vl, sems):
    copies = fetch(((v_hbm, v),), sems)
    x = x_ref[...]
    wide[...] = expand(x, True)
    targets = expand(x, False)
    copies[0].wait()
    vh[...], vl[...] = halves(v[...])
    o_ref[...] = tile_product(targets, wide, vh, vl, step_of(v.shape[0]))


def is_heavy():
    return (lax.axis_index("wide") + lax.axis_index("leaf")) % 2 == 0


def sides():
    partner = 1 - 2 * (lax.axis_index("wide") % 2)
    return partner, -partner


def pair_product_kernel(heavy, a_ref, b_ref, *refs):
    v_refs, (o_ref, wide, vh, vl) = refs[:-4], refs[-4:]

    @pl.when(is_heavy() == heavy)
    def _():
        wide[...] = expand(b_ref[...], True)
        targets = expand(a_ref[...], False)
        start = 0
        for ref in v_refs:
            span = pl.ds(start, ref.shape[0])
            vh[span, :], vl[span, :] = halves(ref[...])
            start += ref.shape[0]
        o_ref[...] = tile_product(targets, wide, vh, vl, step_of(vh.shape[0]))


def far_kernel(count, ids_hbm, count_hbm, own_skels_ref, mate_skels_ref, *refs):
    block_refs, (keep_ref, give_ref, skel_ref, wide, vh, vl, ids_ref, count_ref, sems) = refs[:count], refs[count:]
    copies = fetch(((ids_hbm, ids_ref), (count_hbm, count_ref)), sems)
    cols = keep_ref.shape[1]
    rows = block_refs[0].shape[0]
    parents = lax.axis_size("wide")
    me = lax.axis_index("wide")
    spans = [pl.ds(k * rows, rows) for k in range(count)]
    for k, span in enumerate(spans):
        wide[span, :] = expand(block_refs[k][:, cols:], True)
    core = lax.axis_index("leaf") % 2
    for chip in range(own_skels_ref.shape[1] // rows):
        for ref, place in ((own_skels_ref, core), (mate_skels_ref, 1 - core)):
            span = pl.ds(pl.multiple_of((2 * chip + place) * rows, rows), rows)
            skel_ref[:, span, :] = ref[:, chip * rows : (chip + 1) * rows, :]
    for copy in copies:
        copy.wait()
    heavy = is_heavy()
    for ref, kept in ((keep_ref, True), (give_ref, False)):
        index = jnp.where(heavy == kept, 0, 1)
        target = jnp.where(index == 0, me, me + 1 - 2 * (me % 2))
        for k, span in enumerate(spans):
            other = lax.rem(me - 2 * k + parents, parents)
            wanted = jnp.int32(0)
            for slot in range(ids_ref.shape[1]):
                hit = (ids_ref[target, slot] == other) & (slot < count_ref[target])
                wanted = wanted | hit.astype(jnp.int32)
            vh[span, :], vl[span, :] = halves(jnp.where(wanted > 0, block_refs[k][:, :cols], F32(0.0)))
        ref[...] = tile_product(expand(skel_ref[index], False), wide, vh, vl, step_of(count * rows))


def add_kernel(*refs):
    total = refs[0][...]
    for ref in refs[1:-1]:
        total = total + ref[...]
    refs[-1][...] = total


def lower_kernel(total_ref, rows_ref, t_ref, kept_ref, mate_ref, o_ref):
    field = jnp.where(is_heavy(), kept_ref[...], mate_ref[...])
    o_ref[...] = total_ref[...] + product(rows_ref[...], product(t_ref[0], field))


def last_kernel(ids_ref, count_ref, total_ref, near_ref, far_ref, own_ref, mine_ref, o_hbm, out, sems):
    heavy = is_heavy()
    partner, other = sides()
    to_partner = near_flag(ids_ref, count_ref, partner)
    to_other = near_flag(ids_ref, count_ref, other)
    step = step_of(out.shape[0])
    spans = [pl.ds(k * step, step) for k in range(out.shape[0] // step)]
    stores = [pltpu.make_async_copy(out.at[span, :], o_hbm.at[span, :], sems.at[k]) for k, span in enumerate(spans)]

    def put(first_ref, second_ref):
        for span, store in zip(spans, stores):
            block = total_ref[span, :] + jnp.where(to_partner, first_ref[span, :], F32(0.0))
            out[span, :] = block + jnp.where(to_other, second_ref[span, :], F32(0.0))
            store.start()
        for store in stores:
            store.wait()

    @pl.when(heavy)
    def _():
        put(mine_ref, own_ref)

    @pl.when(jnp.logical_not(heavy))
    def _():
        put(near_ref, far_ref)


VM = pl.BlockSpec(memory_space=pltpu.VMEM)
SM = pl.BlockSpec(memory_space=pltpu.SMEM)
ANY = pl.BlockSpec(memory_space=pl.ANY)
HBM = pl.BlockSpec(memory_space=pltpu.HBM)


def kernel_call(body, out, args, specs, scratch=(), flops=0, out_spec=VM):
    many = isinstance(out[0], tuple)
    outs = out if many else (out,)
    moved = 4 * (sum(a.size for a in args) + sum(math.prod(o) for o in outs))
    shapes = tuple(jax.ShapeDtypeStruct(s, F32) for s in outs)
    return pl.pallas_call(
        body,
        out_shape=shapes if many else shapes[0],
        in_specs=specs,
        out_specs=tuple(out_spec for _ in outs) if many else out_spec,
        scratch_shapes=list(scratch),
        compiler_params=pltpu.CompilerParams(vmem_limit_bytes=VMEM_BYTES),
        cost_estimate=pl.CostEstimate(flops=flops, bytes_accessed=moved, transcendentals=0),
    )(*args)


def sent(block, route):
    return lax.ppermute(block, ("leaf", "wide"), route)


def routes(leaf, wide):
    swap, onward, back, back_far, to_mate = [], [], [], [], []
    for l in range(leaf):
        step = -2 if l % 2 else 2
        for p in range(wide):
            here, mate, partner = l * wide + p, (l ^ 1) * wide + p, l * wide + (p ^ 1)
            if (l + p) % 2:
                swap.append((here, partner))
                continue
            swap.append((here, mate))
            back.append((here, partner))
            to_mate.append((mate, here))
            if 0 <= p + step < wide:
                onward.append((here, mate + step))
            if 0 <= p - step // 2 < wide:
                back_far.append((mate, here - step // 2))
    return swap, onward, back, back_far, to_mate


def shards(rhs, points, order, basis, transfer, skeleton, far_ids, far_count, near_ids, near_count):
    wide = lax.axis_size("wide")
    leaf = lax.axis_size("leaf")
    chips = leaf // 2
    size, cols = rhs.shape
    features = points.shape[1]
    rank = transfer.shape[1]
    rows = rank // leaf
    order = order.reshape(1, size)
    swap, onward, back, back_far, to_mate = routes(leaf, wide)
    all_wide = lambda move: [(l * wide + p, move(l, p)) for l in range(leaf) for p in range(wide)]
    mates = all_wide(lambda l, p: (l ^ 1) * wide + p)
    partners = all_wide(lambda l, p: l * wide + (p ^ 1))
    tile_flops = 2 * size * size * (4 * features + 3 * cols)
    dma = pltpu.SemaphoreType.DMA
    spot_buf, rhs_buf = pltpu.VMEM((size, features), F32), pltpu.VMEM((size, cols), F32)
    scratch = [pltpu.VMEM((size, 4 * features), BF), pltpu.VMEM((size, cols), BF), pltpu.VMEM((size, cols), BF)]

    def across_chips(blocks, senders):
        moves = [all_wide(lambda l, p: ((l // 2 + shift) % chips * 2 + l % 2) * wide + p) for shift in range(1, chips)]
        return [sent(block, [pair for pair in move if pair[0] in senders]) for block, move in zip(blocks, moves)]

    def pair_product(heavy, a, b, *v):
        return kernel_call(
            functools.partial(pair_product_kernel, heavy), (size, cols), (a, b) + v, [VM] * (2 + len(v)),
            scratch, tile_flops,
        )

    half = size // 2
    skel_next = sent(skeleton[0], partners)
    rhs_a = kernel_call(
        first_kernel, (size // 2, cols), (pltpu.with_memory_space_constraint(rhs, pltpu.HBM),), [HBM], [dma((1,))]
    )
    spots, basis_rows, term, rhs_b = kernel_call(
        front_kernel, ((size, features), (size, rank), (rank, cols), (size - half, cols)),
        tuple(pltpu.with_memory_space_constraint(t, pltpu.HBM) for t in (order, points, basis, rhs, transfer)),
        [HBM] * 5,
        [pltpu.VMEM((1, size), jnp.int32), spot_buf, pltpu.VMEM((size, rank), F32), rhs_buf, pltpu.VMEM(transfer.shape, F32), dma((5,))],
        4 * size * size * (rank + features),
    )
    mate_term = sent(term, mates)
    spots_in = sent(spots, swap)
    kept, *sends = kernel_call(
        chip_kernel, ((rows, cols + 2 * features),) * chips, (term, mate_term, skeleton, skel_next), [VM] * 4
    )
    received = across_chips(sends, range(leaf * wide))
    total = kernel_call(self_kernel, (size, cols), (spots, rhs), [VM, ANY], [rhs_buf] + scratch + [dma((1,))], tile_flops)
    block, skels = kernel_call(
        gather_kernel, ((rows, cols + features), (2, chips * rows, features)), (kept, *received), [VM] * chips
    )
    mate_skels = sent(skels, mates)
    rhs_in = (sent(rhs_a, swap), sent(rhs_b, swap))
    spots_far = sent(spots_in, onward)
    blocks = [block] + [sent(block, all_wide(lambda l, p: l * wide + (p + 2 * k) % wide)) for k in range(1, wide // 2)]
    share_near = sent(pair_product(True, spots_in, spots, rhs), back)
    share_far = sent(pair_product(False, spots_far, spots_in, *rhs_in), back_far)
    rhs_far = (sent(rhs_in[0], onward), sent(rhs_in[1], onward))
    mine = pair_product(True, spots, spots_in, *rhs_in)
    sources = len(blocks) * rows
    keep, give = kernel_call(
        functools.partial(far_kernel, len(blocks)), ((rank, cols),) * 2,
        (pltpu.with_memory_space_constraint(far_ids, pltpu.HBM), pltpu.with_memory_space_constraint(far_count, pltpu.HBM), skels, mate_skels, *blocks),
        [HBM, HBM] + [VM] * (2 + len(blocks)),
        [pltpu.VMEM((2, rank, features), F32), pltpu.VMEM((sources, 4 * features), BF), pltpu.VMEM((sources, cols), BF), pltpu.VMEM((sources, cols), BF)]
        + [pltpu.SMEM(far_ids.shape, jnp.int32), pltpu.SMEM(far_count.shape, jnp.int32), dma((2,))],
        4 * rank * sources * (4 * features + 3 * cols),
    )

    def added(*terms):
        return kernel_call(add_kernel, (rank, cols), terms, [VM] * len(terms))

    heavies = [here for here, _ in back]
    keep = added(keep, sent(give, mates))
    keep = added(keep, sent(keep, [(there, here) for here, there in back]))
    fields = across_chips([keep] * (chips - 1), heavies)
    field = added(keep, *fields)
    mate_field = sent(field, mates)
    own_far = sent(pair_product(False, spots_in, spots_far, *rhs_far), to_mate)
    total = kernel_call(
        lower_kernel, (size, cols), (total, basis_rows, transfer, field, mate_field), [VM] * 5, (),
        6 * size * rank * cols,
    )
    return kernel_call(
        last_kernel, (size, cols), (near_ids, near_count, total, share_near, share_far, own_far, mine),
        [SM, SM] + [VM] * 5, [rhs_buf, dma((size // step_of(size),))], size * cols, ANY,
    )


def solution(mesh):
    placed = (
        P(("leaf", "wide"), None),
        P(("leaf", "wide"), None),
        P(("leaf", "wide")),
        P(("leaf", "wide"), None),
        P(("leaf", "wide"), None, None),
        P("wide", "leaf", None),
        P(),
        P(),
        P(("leaf", "wide"), None),
        P(("leaf", "wide")),
    )
    return jax.shard_map(shards, mesh=mesh, in_specs=placed, out_specs=P(("leaf", "wide"), None), check_vma=False)
```

```python
import functools
import math

import jax
import jax.numpy as jnp
from jax import lax
from jax.experimental import pallas as pl
from jax.experimental.pallas import tpu as pltpu
from jax.sharding import PartitionSpec as P

BF = jnp.bfloat16
F32 = jnp.float32
VMEM_BYTES = 28 << 20


def halves(x):
    hi = x.astype(BF)
    return hi, (x - hi.astype(F32)).astype(BF)


def expand(x, second):
    features = x.shape[1]
    hi, lo = halves(x * F32(math.sqrt(4.0 / features * math.log2(math.e))))
    hi_wide = hi.astype(F32)
    norm = jnp.sum(hi_wide * (hi_wide * 0.5 + lo.astype(F32)), axis=1, keepdims=True) * -1.0
    a = norm.astype(BF).astype(F32)
    b = (norm - a).astype(BF).astype(F32)
    c = norm - a - b
    lane = lax.broadcasted_iota(jnp.int32, x.shape, 1)
    k = 3 if second else 0
    ones = jnp.where(lane < 6, F32(1.0), F32(0.0))
    ext = jnp.where(lane == k, a, jnp.where(lane == k + 1, b, jnp.where(lane == k + 2, c, ones))).astype(BF)
    return jnp.concatenate([hi, hi, lo, ext] if second else [hi, lo, hi, ext], axis=1)


def dot(left, right):
    return lax.dot_general(left, right, (((1,), (0,)), ((), ())), preferred_element_type=F32)


def dot_last(left, right):
    return lax.dot_general(left, right, (((1,), (1,)), ((), ())), preferred_element_type=F32)


def dot_first(left, right):
    return lax.dot_general(left, right, (((0,), (0,)), ((), ())), preferred_element_type=F32)


def product(left, right, op=dot):
    lh, ll = halves(left)
    rh, rl = halves(right)
    return op(lh, rh) + op(ll, rh) + op(lh, rl)


def tile_product(targets, sources, value_hi, value_lo, step):
    total = None
    for start in range(0, sources.shape[0], step):
        span = pl.ds(start, step)
        hi, lo = halves(jnp.exp2(dot_last(targets, sources[span, :])))
        part = dot(hi, value_hi[span, :]) + dot(lo, value_hi[span, :]) + dot(hi, value_lo[span, :])
        total = part if total is None else total + part
    return total


def step_of(count):
    return 256 if count % 256 == 0 else count


def near_flag(near_ids, near_count, offset):
    wide = lax.axis_size("wide")
    wanted = lax.axis_index("leaf") * wide + lax.axis_index("wide") + offset
    found = jnp.int32(0)
    for slot in range(near_ids.shape[1]):
        hit = (near_ids[0, slot] == wanted) & (slot < near_count[0])
        found = found | hit.astype(jnp.int32)
    return found > 0


def hot_rows(order_ref):
    n = order_ref.shape[1]
    row = lax.broadcasted_iota(jnp.int32, (n, n), 0)
    return jnp.where(row == order_ref[...], F32(1.0), F32(0.0)).astype(BF)


def fetch(pairs, sems):
    copies = [pltpu.make_async_copy(src, dst, sems.at[k]) for k, (src, dst) in enumerate(pairs)]
    for copy in copies:
        copy.start()
    return copies


def front_kernel(order_hbm, x_hbm, w_hbm, v_hbm, t_hbm, spots_ref, rows_ref, sum_ref, va_ref, vb_ref, order_ref, x, w, v, t, sems):
    first, *copies = fetch(
        ((order_hbm, order_ref), (x_hbm, x), (w_hbm, w), (v_hbm, v), (t_hbm, t)), sems
    )
    first.wait()
    hot = hot_rows(order_ref)
    width = x.shape[1]
    copies[0].wait()
    hi, lo = halves(x[...])
    both = dot(hot, jnp.concatenate([hi, lo], axis=1))
    spots_ref[...] = both[:, :width] + both[:, width:]
    copies[1].wait()
    hi, lo = halves(w[...])
    rows = dot(hot, hi)
    rows_lo = dot(hot, lo)
    rows_ref[...] = rows + rows_lo
    rh, rl = rows.astype(BF), rows_lo.astype(BF)
    copies[2].wait()
    half = va_ref.shape[0]
    va_ref[...] = v[:half, :]
    vb_ref[...] = v[half:, :]
    vh, vl = halves(v[...])
    coef = dot_first(rh, vh) + dot_first(rl, vh) + dot_first(rh, vl)
    copies[3].wait()
    sum_ref[...] = product(t[0], coef, dot_first)


def chip_kernel(own_ref, mate_ref, skel_ref, next_ref, keep_ref, *send_refs):
    leaf = lax.axis_index("leaf")
    chips = len(send_refs) + 1
    features = next_ref.shape[1]
    cols = own_ref.shape[1]
    block = keep_ref.shape[0]
    for shift, ref in enumerate((keep_ref,) + send_refs):
        chip = lax.rem(leaf // 2 + shift, chips)
        span = pl.ds(pl.multiple_of((2 * chip + leaf % 2) * block, block), block)
        ref[:, :cols] = own_ref[span, :] + mate_ref[span, :]
        ref[:, cols : cols + features] = skel_ref[0]
        ref[:, cols + features :] = next_ref[...]


def gather_kernel(*refs):
    received, (block_ref, skels_ref) = refs[:-2], refs[-2:]
    leaf = lax.axis_index("leaf")
    chips = len(received)
    features = skels_ref.shape[2]
    cols = block_ref.shape[1] - features
    block = block_ref.shape[0]
    total = received[0][:, :cols]
    for ref in received[1:]:
        total = total + ref[:, :cols]
    block_ref[:, :cols] = total
    block_ref[:, cols:] = received[0][:, cols : cols + features]
    for shift, ref in enumerate(received):
        chip = lax.rem(leaf // 2 - shift + chips, chips)
        span = pl.ds(pl.multiple_of(chip * block, block), block)
        for k in range(2):
            skels_ref[k, span, :] = ref[:, cols + k * features : cols + (k + 1) * features]


def self_kernel(x_ref, v_hbm, o_ref, v, wide, vh, vl, sems):
    copies = fetch(((v_hbm, v),), sems)
    x = x_ref[...]
    wide[...] = expand(x, True)
    targets = expand(x, False)
    copies[0].wait()
    vh[...], vl[...] = halves(v[...])
    o_ref[...] = tile_product(targets, wide, vh, vl, step_of(v.shape[0]))


def is_heavy():
    return (lax.axis_index("wide") + lax.axis_index("leaf")) % 2 == 0


def sides():
    partner = 1 - 2 * (lax.axis_index("wide") % 2)
    return partner, -partner


def pair_product_kernel(heavy, a_ref, b_ref, *refs):
    v_refs, (o_ref, wide, vh, vl) = refs[:-4], refs[-4:]

    @pl.when(is_heavy() == heavy)
    def _():
        wide[...] = expand(b_ref[...], True)
        targets = expand(a_ref[...], False)
        start = 0
        for ref in v_refs:
            span = pl.ds(start, ref.shape[0])
            vh[span, :], vl[span, :] = halves(ref[...])
            start += ref.shape[0]
        o_ref[...] = tile_product(targets, wide, vh, vl, step_of(vh.shape[0]))


def far_kernel(count, ids_hbm, count_hbm, own_skels_ref, mate_skels_ref, *refs):
    block_refs, (keep_ref, give_ref, skel_ref, wide, vh, vl, ids_ref, count_ref, sems) = refs[:count], refs[count:]
    copies = fetch(((ids_hbm, ids_ref), (count_hbm, count_ref)), sems)
    cols = keep_ref.shape[1]
    rows = block_refs[0].shape[0]
    parents = lax.axis_size("wide")
    me = lax.axis_index("wide")
    spans = [pl.ds(k * rows, rows) for k in range(count)]
    for k, span in enumerate(spans):
        wide[span, :] = expand(block_refs[k][:, cols:], True)
    core = lax.axis_index("leaf") % 2
    for chip in range(own_skels_ref.shape[1] // rows):
        for ref, place in ((own_skels_ref, core), (mate_skels_ref, 1 - core)):
            span = pl.ds(pl.multiple_of((2 * chip + place) * rows, rows), rows)
            skel_ref[:, span, :] = ref[:, chip * rows : (chip + 1) * rows, :]
    for copy in copies:
        copy.wait()
    heavy = is_heavy()
    for ref, kept in ((keep_ref, True), (give_ref, False)):
        index = jnp.where(heavy == kept, 0, 1)
        target = jnp.where(index == 0, me, me + 1 - 2 * (me % 2))
        for k, span in enumerate(spans):
            other = lax.rem(me - 2 * k + parents, parents)
            wanted = jnp.int32(0)
            for slot in range(ids_ref.shape[1]):
                hit = (ids_ref[target, slot] == other) & (slot < count_ref[target])
                wanted = wanted | hit.astype(jnp.int32)
            vh[span, :], vl[span, :] = halves(jnp.where(wanted > 0, block_refs[k][:, :cols], F32(0.0)))
        ref[...] = tile_product(expand(skel_ref[index], False), wide, vh, vl, step_of(count * rows))


def add_kernel(*refs):
    total = refs[0][...]
    for ref in refs[1:-1]:
        total = total + ref[...]
    refs[-1][...] = total


def lower_kernel(total_ref, rows_ref, t_ref, kept_ref, mate_ref, o_ref):
    field = jnp.where(is_heavy(), kept_ref[...], mate_ref[...])
    o_ref[...] = total_ref[...] + product(rows_ref[...], product(t_ref[0], field))


def last_kernel(ids_ref, count_ref, total_ref, near_ref, far_ref, own_ref, mine_ref, o_hbm, out, sems):
    heavy = is_heavy()
    partner, other = sides()
    to_partner = near_flag(ids_ref, count_ref, partner)
    to_other = near_flag(ids_ref, count_ref, other)
    step = step_of(out.shape[0])
    spans = [pl.ds(k * step, step) for k in range(out.shape[0] // step)]
    stores = [pltpu.make_async_copy(out.at[span, :], o_hbm.at[span, :], sems.at[k]) for k, span in enumerate(spans)]

    def put(first_ref, second_ref):
        for span, store in zip(spans, stores):
            block = total_ref[span, :] + jnp.where(to_partner, first_ref[span, :], F32(0.0))
            out[span, :] = block + jnp.where(to_other, second_ref[span, :], F32(0.0))
            store.start()
        for store in stores:
            store.wait()

    @pl.when(heavy)
    def _():
        put(mine_ref, own_ref)

    @pl.when(jnp.logical_not(heavy))
    def _():
        put(near_ref, far_ref)


VM = pl.BlockSpec(memory_space=pltpu.VMEM)
SM = pl.BlockSpec(memory_space=pltpu.SMEM)
ANY = pl.BlockSpec(memory_space=pl.ANY)
HBM = pl.BlockSpec(memory_space=pltpu.HBM)


def kernel_call(body, out, args, specs, scratch=(), flops=0, out_spec=VM):
    many = isinstance(out[0], tuple)
    outs = out if many else (out,)
    moved = 4 * (sum(a.size for a in args) + sum(math.prod(o) for o in outs))
    shapes = tuple(jax.ShapeDtypeStruct(s, F32) for s in outs)
    return pl.pallas_call(
        body,
        out_shape=shapes if many else shapes[0],
        in_specs=specs,
        out_specs=tuple(out_spec for _ in outs) if many else out_spec,
        scratch_shapes=list(scratch),
        compiler_params=pltpu.CompilerParams(vmem_limit_bytes=VMEM_BYTES),
        cost_estimate=pl.CostEstimate(flops=flops, bytes_accessed=moved, transcendentals=0),
    )(*args)


def sent(block, route):
    return lax.ppermute(block, ("leaf", "wide"), route)


def routes(leaf, wide):
    swap, onward, back, back_far, to_mate = [], [], [], [], []
    for l in range(leaf):
        step = -2 if l % 2 else 2
        for p in range(wide):
            here, mate, partner = l * wide + p, (l ^ 1) * wide + p, l * wide + (p ^ 1)
            if (l + p) % 2:
                swap.append((here, partner))
                continue
            swap.append((here, mate))
            back.append((here, partner))
            to_mate.append((mate, here))
            if 0 <= p + step < wide:
                onward.append((here, mate + step))
            if 0 <= p - step // 2 < wide:
                back_far.append((mate, here - step // 2))
    return swap, onward, back, back_far, to_mate


def shards(rhs, points, order, basis, transfer, skeleton, far_ids, far_count, near_ids, near_count):
    wide = lax.axis_size("wide")
    leaf = lax.axis_size("leaf")
    chips = leaf // 2
    size, cols = rhs.shape
    features = points.shape[1]
    rank = transfer.shape[1]
    rows = rank // leaf
    order = order.reshape(1, size)
    swap, onward, back, back_far, to_mate = routes(leaf, wide)
    all_wide = lambda move: [(l * wide + p, move(l, p)) for l in range(leaf) for p in range(wide)]
    mates = all_wide(lambda l, p: (l ^ 1) * wide + p)
    partners = all_wide(lambda l, p: l * wide + (p ^ 1))
    tile_flops = 2 * size * size * (4 * features + 3 * cols)
    dma = pltpu.SemaphoreType.DMA
    spot_buf, rhs_buf = pltpu.VMEM((size, features), F32), pltpu.VMEM((size, cols), F32)
    scratch = [pltpu.VMEM((size, 4 * features), BF), pltpu.VMEM((size, cols), BF), pltpu.VMEM((size, cols), BF)]

    def across_chips(blocks, senders):
        moves = [all_wide(lambda l, p: ((l // 2 + shift) % chips * 2 + l % 2) * wide + p) for shift in range(1, chips)]
        return [sent(block, [pair for pair in move if pair[0] in senders]) for block, move in zip(blocks, moves)]

    def pair_product(heavy, a, b, *v):
        return kernel_call(
            functools.partial(pair_product_kernel, heavy), (size, cols), (a, b) + v, [VM] * (2 + len(v)),
            scratch, tile_flops,
        )

    half = size // 2
    skel_next = sent(skeleton[0], partners)
    spots, basis_rows, term, rhs_a, rhs_b = kernel_call(
        front_kernel, ((size, features), (size, rank), (rank, cols), (half, cols), (size - half, cols)),
        tuple(pltpu.with_memory_space_constraint(t, pltpu.HBM) for t in (order, points, basis, rhs, transfer)),
        [HBM] * 5,
        [pltpu.VMEM((1, size), jnp.int32), spot_buf, pltpu.VMEM((size, rank), F32), rhs_buf, pltpu.VMEM(transfer.shape, F32), dma((5,))],
        4 * size * size * (rank + features),
    )
    mate_term = sent(term, mates)
    spots_in = sent(spots, swap)
    kept, *sends = kernel_call(
        chip_kernel, ((rows, cols + 2 * features),) * chips, (term, mate_term, skeleton, skel_next), [VM] * 4
    )
    received = across_chips(sends, range(leaf * wide))
    total = kernel_call(self_kernel, (size, cols), (spots, rhs), [VM, ANY], [rhs_buf] + scratch + [dma((1,))], tile_flops)
    block, skels = kernel_call(
        gather_kernel, ((rows, cols + features), (2, chips * rows, features)), (kept, *received), [VM] * chips
    )
    mate_skels = sent(skels, mates)
    rhs_in = (sent(rhs_a, swap), sent(rhs_b, swap))
    spots_far = sent(spots_in, onward)
    blocks = [block] + [sent(block, all_wide(lambda l, p: l * wide + (p + 2 * k) % wide)) for k in range(1, wide // 2)]
    share_near = sent(pair_product(True, spots_in, spots, rhs), back)
    share_far = sent(pair_product(False, spots_far, spots_in, *rhs_in), back_far)
    rhs_far = (sent(rhs_in[0], onward), sent(rhs_in[1], onward))
    mine = pair_product(True, spots, spots_in, *rhs_in)
    sources = len(blocks) * rows
    keep, give = kernel_call(
        functools.partial(far_kernel, len(blocks)), ((rank, cols),) * 2,
        (pltpu.with_memory_space_constraint(far_ids, pltpu.HBM), pltpu.with_memory_space_constraint(far_count, pltpu.HBM), skels, mate_skels, *blocks),
        [HBM, HBM] + [VM] * (2 + len(blocks)),
        [pltpu.VMEM((2, rank, features), F32), pltpu.VMEM((sources, 4 * features), BF), pltpu.VMEM((sources, cols), BF), pltpu.VMEM((sources, cols), BF)]
        + [pltpu.SMEM(far_ids.shape, jnp.int32), pltpu.SMEM(far_count.shape, jnp.int32), dma((2,))],
        4 * rank * sources * (4 * features + 3 * cols),
    )

    def added(*terms):
        return kernel_call(add_kernel, (rank, cols), terms, [VM] * len(terms))

    heavies = [here for here, _ in back]
    keep = added(keep, sent(give, mates))
    keep = added(keep, sent(keep, [(there, here) for here, there in back]))
    fields = across_chips([keep] * (chips - 1), heavies)
    field = added(keep, *fields)
    mate_field = sent(field, mates)
    own_far = sent(pair_product(False, spots_in, spots_far, *rhs_far), to_mate)
    total = kernel_call(
        lower_kernel, (size, cols), (total, basis_rows, transfer, field, mate_field), [VM] * 5, (),
        6 * size * rank * cols,
    )
    return kernel_call(
        last_kernel, (size, cols), (near_ids, near_count, total, share_near, share_far, own_far, mine),
        [SM, SM] + [VM] * 5, [rhs_buf, dma((size // step_of(size),))], size * cols, ANY,
    )


def solution(mesh):
    placed = (
        P(("leaf", "wide"), None),
        P(("leaf", "wide"), None),
        P(("leaf", "wide")),
        P(("leaf", "wide"), None),
        P(("leaf", "wide"), None, None),
        P("wide", "leaf", None),
        P(),
        P(),
        P(("leaf", "wide"), None),
        P(("leaf", "wide")),
    )
    return jax.shard_map(shards, mesh=mesh, in_specs=placed, out_specs=P(("leaf", "wide"), None), check_vma=False)
```
